32 devices in a mesh: batch: 16 (over z, y, core), tm: 2 (over x).
Axes of the slice: x: 2, y: 2, z: 4, core: 2. Of those that a mesh axis runs over, the one named last changes fastest.
Arguments:
- ref_rows: bfloat16 [8192, 1024], P(('batch', 'tm')), may hold values from -6 to 6
- neg_rows: bfloat16 [2048, 1024], P(('batch', 'tm')), may hold values from -6 to 6
- recording: bfloat16 [1024, 1024], P('tm'), may hold values from -6 to 6
- pos_owner: int32 [8192, 1], P(('batch', 'tm')), may hold values from 0 to 1; in each aligned block of 256 rows (0 to 255, 256 to 511, ...) at most 256 rows name the same one
- pos_row: int32 [8192], P(('batch', 'tm')), may hold values from 0 to 511
- ref_animal: int32 [8192], P(('batch', 'tm')), may hold values from 0 to 7
- neg_animal: int32 [2048], P(('batch', 'tm')), may hold values from 0 to 7
- w_in: bfloat16 [1024, 512], replicated, may hold values from -0.1875 to 0.1875
- bias_animal: float32 [8, 512], replicated, may hold values from -5 to 5
- w_out: bfloat16 [512, 128], replicated, may hold values from -0.25 to 0.25
Outputs:
- ref_loss: float32 [8192], P(('batch', 'tm'))
- grad_w_in: bfloat16 [1024, 512], replicated
- grad_w_out: float32 [512, 128], replicated
- grad_bias: float32 [8, 512], replicated
The draws below stay inside these ranges and needn't reach their ends.
Inputs may be any that keep to these rules, and one draw needn't show every extreme that they name: `pos_owner`: among the 256 references of one device at most 256 name one owner, and in every draw some owner is named by exactly 256 of them.
All inputs are finite; a program needn't handle non-finite values.
Results may differ from the reference program's by a relative error of at most 0.0069.
Values may be sent and summed in bfloat16 or wider, within the bound.
No kernel may reach another device: no remote copies, remote signals or barrier semaphores. Data moves between devices by JAX's collectives and lax.ppermute only.
A program may use at most 64 MiB of HBM per device.

```python
import math
import jax
import jax.numpy as jnp
import numpy as np
from jax import lax

C = 1024
H = 512
E = 128
ANIMALS = 8
REF_DEV = 256
NEG_DEV = 64
S_DEV = 512
CAP = 256
ANCHOR_COUNT = 8192
NEGS = 2048
SAMPLES = 1024
N_BATCH = 16
N_TM = 2


def touch_ends(entries, own_key, smallest, top_value):
    index_at = [jax.random.randint(jax.random.fold_in(own_key, axis), (), 0, length) for axis, length in enumerate(entries.shape)]
    main_axis = entries.shape.index(max(entries.shape))
    beside = index_at[:main_axis] + [(index_at[main_axis] + 1) % entries.shape[main_axis]] + index_at[main_axis + 1:]
    return entries.at[tuple(index_at)].set(smallest).at[tuple(beside)].set(top_value)


def block_scale(stream_key, extent, shards, least, top_value):
    gain = 1.0
    for position, blocks in shards:
        steps = jax.random.uniform(jax.random.fold_in(jax.random.fold_in(stream_key, 6), position), (blocks,), jnp.float32, least / len(shards), top_value / len(shards))
        gain = gain * jnp.repeat(jnp.exp(steps), extent[position] // blocks).reshape((-1,) + (1,) * (len(extent) - 1 - position))
    return gain


def routed_block(own_key, own, number, rows, count, top, limit, skew):
    order = jax.random.permutation(own_key, count)
    packed, common = load_shares(count, rows * top, limit, skew, True), load_shares(count, rows * top, limit, skew, False)
    places = jnp.arange(count)

    def named(tallies, rotation):
        used = int((tallies > 0).sum())
        fixed = max(1, used // 4)
        moved = fixed + (places - fixed + rotation * (used - fixed)) % max(1, count - fixed)
        return jnp.zeros((count,), jnp.int32).at[order[jnp.where(places < fixed, places, moved)]].set(jnp.asarray(tallies, jnp.int32))

    tallies = jnp.where(number % 4 == 0, named(packed, number // 4), named(common, number - number // 4 - 1))
    mixed = jax.random.permutation(jax.random.fold_in(own, 3), count)
    giver, sink = mixed[0:count // 2 * 2:2], mixed[1:count // 2 * 2:2]
    margin = jnp.minimum(tallies[giver] - 1, limit - tallies[sink]) // 2
    margin = jnp.where((giver == order[0]) | (sink == order[0]) | (tallies[sink] == 0), 0, jnp.maximum(margin, 0))
    moved = jax.random.randint(jax.random.fold_in(own, 4), (count // 2,), 0, 1 << 20) % (margin + 1)
    tallies = tallies.at[giver].add(-moved).at[sink].add(moved)
    members = jnp.searchsorted(jnp.cumsum(tallies), jnp.arange(rows * top), side="right").astype(jnp.int32)
    grid = members.reshape(top, rows).T
    grid = grid[jax.random.permutation(jax.random.fold_in(own, 1), rows)]
    rotation = jax.random.randint(jax.random.fold_in(own, 2), (rows, 1), 0, top)
    return jnp.take_along_axis(grid, (jnp.arange(top)[None, :] + rotation) % top, axis=1)


def load_shares(count, total, most, skew, full):
    portions = [(1 << 20) // math.isqrt(standing ** skew) + 1 for standing in range(1, count + 1)]
    largest = most if full else min(most, max(-(-total // count), total * portions[0] // sum(portions)))
    least = 1 if total - largest >= count - 1 else 0
    given, rest = [largest] + [least] * (count - 1), total - largest - least * (count - 1)
    while rest > 0:
        movable = [i for i in range(1, count) if given[i] < largest] or [i for i in range(1, count) if given[i] < most]
        mass, left = sum([portions[i] for i in movable]), rest
        for i in movable:
            extra = min(most - given[i], max(1, left * portions[i] // mass), rest)
            given[i] = given[i] + extra
            rest = rest - extra
    return np.array(given)


def centred(key, shape, deviation, bound, split=(), held_as=jnp.bfloat16):
    gain = block_scale(key, shape, split, -0.22, 0.18) if split else 1.0
    array = jax.random.normal(key, shape, jnp.float32) * deviation * gain
    return jnp.minimum(jnp.maximum(array, -bound), bound).astype(held_as)


def setup_inputs(seed: int = 0) -> dict:
    keys = jax.random.split(jax.random.key(seed), 11)
    ref_rows = centred(keys[0], (ANCHOR_COUNT, C), 1.0, 6.0, ((0, 32),))
    neg_rows = centred(keys[1], (NEGS, C), 1.0, 6.0, ((0, 32),))
    recording = centred(keys[2], (SAMPLES, C), 1.0, 6.0, ((0, 2),))
    pos_owner_keys = jax.random.split(jax.random.fold_in(keys[3], 1), ANCHOR_COUNT // REF_DEV)
    pos_owner_turns = jax.random.permutation(jax.random.fold_in(keys[3], 3), ANCHOR_COUNT // REF_DEV)
    pos_owner = jax.vmap(lambda own, number: routed_block(jax.random.fold_in(keys[3], 2), own, number, REF_DEV, N_TM, 1, CAP, 2))(pos_owner_keys, pos_owner_turns).reshape((ANCHOR_COUNT, 1))
    pos_row = touch_ends(jax.random.randint(keys[4], (ANCHOR_COUNT,), 0, S_DEV), jax.random.fold_in(keys[4], 1), 0, S_DEV - 1).astype(jnp.int32)
    ref_animal = touch_ends(jax.random.randint(keys[5], (ANCHOR_COUNT,), 0, ANIMALS), jax.random.fold_in(keys[5], 1), 0, ANIMALS - 1).astype(jnp.int32)
    neg_animal = touch_ends(jax.random.randint(keys[6], (NEGS,), 0, ANIMALS), jax.random.fold_in(keys[6], 1), 0, ANIMALS - 1).astype(jnp.int32)
    w_in = centred(keys[7], (C, H), C ** -0.5, 0.1875)
    bias_animal = centred(keys[8], (ANIMALS, H), 1.0, 5.0, (), jnp.float32)
    w_out = centred(keys[9], (H, E), H ** -0.5, 0.25)
    return {"ref_rows": ref_rows, "neg_rows": neg_rows, "recording": recording, "pos_owner": pos_owner, "pos_row": pos_row, "ref_animal": ref_animal, "neg_animal": neg_animal, "w_in": w_in, "bias_animal": bias_animal, "w_out": w_out}


logit_sharpness_divisor = 0.1
shift_bound = 10.0
epsilon = 1e-06

def encode_rows(samples, animal_ids, w_in, bias_animal, w_out):
    pre_act = jnp.dot(samples, w_in, preferred_element_type=jnp.float32) + bias_animal[animal_ids]
    hidden = jax.nn.gelu(pre_act).astype(jnp.bfloat16)
    latent = jnp.dot(hidden, w_out, preferred_element_type=jnp.float32)
    radius = jnp.sqrt(lax.optimization_barrier(jnp.sum(latent * latent, axis=1, keepdims=True)) + epsilon)
    unit_vec = (latent / radius).astype(jnp.bfloat16)
    return (pre_act, hidden, latent, radius, unit_vec)

def backward_rows(samples, animal_ids, pre_act, hidden, latent, radius, grad_unit, w_out):
    inner = lax.optimization_barrier(jnp.sum(latent * grad_unit, axis=1, keepdims=True))
    grad_latent = ((grad_unit - latent * inner / (radius * radius)) / radius).astype(jnp.bfloat16)
    grad_hidden = jnp.dot(grad_latent, w_out.T, preferred_element_type=jnp.float32)
    grad_pre = jax.vjp(jax.nn.gelu, pre_act)[1](grad_hidden)[0].astype(jnp.bfloat16)
    grad_out = jnp.dot(hidden.T, grad_latent, preferred_element_type=jnp.float32)
    grad_in = jnp.dot(samples.T, grad_pre, preferred_element_type=jnp.float32)
    grad_bias = jax.ops.segment_sum(grad_pre.astype(jnp.float32), animal_ids, ANIMALS)
    return (grad_out, grad_in, grad_bias)

def by_column(values, per_block):
    return values.reshape(N_BATCH, N_TM, per_block, -1).transpose(1, 0, 2, 3).reshape(N_TM, N_BATCH * per_block, -1)

def from_column(values, per_block):
    return values.reshape(N_TM, N_BATCH, per_block, -1).transpose(1, 0, 2, 3).reshape(N_BATCH * N_TM * per_block, -1)

def column_terms(operands):
    normalized_entries, matching_entries, distractor_entries = operands
    matching_similarity = lax.optimization_barrier(jnp.sum(normalized_entries.astype(jnp.float32) * matching_entries.astype(jnp.float32), axis=1)) / logit_sharpness_divisor
    similarity_table = jnp.dot(normalized_entries, distractor_entries.T, preferred_element_type=jnp.float32) / logit_sharpness_divisor
    exponent = jnp.exp(similarity_table - shift_bound)
    normalizer = jnp.exp(matching_similarity - shift_bound) + lax.optimization_barrier(jnp.sum(exponent, axis=1))
    loss_col = jnp.log(normalizer) + shift_bound - matching_similarity
    weights = (exponent / normalizer[:, None]).astype(jnp.bfloat16)
    pos_prob = jnp.exp(matching_similarity - shift_bound) / normalizer
    reciprocal_factor = ANCHOR_COUNT ** (-0.5) / logit_sharpness_divisor
    grad_ref = reciprocal_factor * (jnp.dot(weights, distractor_entries, preferred_element_type=jnp.float32) + (pos_prob - 1.0)[:, None] * matching_entries.astype(jnp.float32))
    grad_pos = reciprocal_factor * (pos_prob - 1.0)[:, None] * normalized_entries.astype(jnp.float32)
    grad_neg = reciprocal_factor * jnp.dot(weights.T, normalized_entries, preferred_element_type=jnp.float32)
    return (loss_col, grad_ref, grad_pos, grad_neg)

def reference(ref_rows, neg_rows, recording, pos_owner, pos_row, ref_animal, neg_animal, w_in, bias_animal, w_out):
    sample_index = (pos_owner[:, 0] * S_DEV + pos_row).astype(jnp.int32)
    pos_rows = recording[sample_index]
    ref_enc = encode_rows(ref_rows, ref_animal, w_in, bias_animal, w_out)
    pos_enc = encode_rows(pos_rows, ref_animal, w_in, bias_animal, w_out)
    neg_enc = encode_rows(neg_rows, neg_animal, w_in, bias_animal, w_out)
    operands = (by_column(ref_enc[4], REF_DEV), by_column(pos_enc[4], REF_DEV), by_column(neg_enc[4], NEG_DEV))
    loss_col, grad_ref, grad_pos, grad_neg = lax.map(column_terms, operands)
    ref_loss = from_column(loss_col[:, :, None], REF_DEV)[:, 0]
    grad_ref = from_column(grad_ref, REF_DEV)
    grad_pos = from_column(grad_pos, REF_DEV)
    grad_neg = from_column(grad_neg, NEG_DEV)
    parts_a = backward_rows(ref_rows, ref_animal, ref_enc[0], ref_enc[1], ref_enc[2], ref_enc[3], grad_ref, w_out)
    parts_b = backward_rows(pos_rows, ref_animal, pos_enc[0], pos_enc[1], pos_enc[2], pos_enc[3], grad_pos, w_out)
    parts_c = backward_rows(neg_rows, neg_animal, neg_enc[0], neg_enc[1], neg_enc[2], neg_enc[3], grad_neg, w_out)
    grad_w_out = parts_a[0] + parts_b[0] + parts_c[0]
    grad_w_in = (parts_a[1] + parts_b[1] + parts_c[1]).astype(jnp.bfloat16)
    grad_bias = parts_a[2] + parts_b[2] + parts_c[2]
    return (ref_loss, grad_w_in, grad_w_out, grad_bias)
```

```python
import jax
import jax.numpy as jnp
from jax import lax
from jax.sharding import PartitionSpec as P

logit_sharpness_divisor = 0.1
shift_bound = 10.0
epsilon = 1e-06
AXES = ("batch", "tm")
bf16 = jnp.bfloat16
f32 = jnp.float32


def swap(x, axes, mask, n):
    return lax.ppermute(x, axes, [(i, i ^ mask) for i in range(n)])


def batch_masks(nb):
    return [1 << i for i in range(nb.bit_length() - 1)]


def gather_batch(x, nb, me):
    masks = batch_masks(nb)
    order = masks[2:][::-1] + masks[1:2] + masks[:1]
    rows = x.shape[0]
    parts = {0: x}
    for m in order:
        keys = list(parts)
        block = jnp.concatenate([parts[k] for k in keys], 0) if len(keys) > 1 else parts[keys[0]]
        got = swap(block, "batch", m, nb)
        for i, k in enumerate(keys):
            parts[k ^ m] = got[i * rows : (i + 1) * rows]
    out = jnp.zeros((nb,) + x.shape, x.dtype)
    for k, part in parts.items():
        out = lax.dynamic_update_index_in_dim(out, part, me ^ k, 0)
    return out.reshape((nb * rows,) + x.shape[1:])


def scatter_batch(x, nb, me):
    masks = batch_masks(nb)
    order = masks[:1] + masks[1:][::-1]
    xs = x.reshape((nb, x.shape[0] // nb) + x.shape[1:])
    parts = {k: lax.dynamic_index_in_dim(xs, me ^ k, 0, False) for k in range(nb)}
    for m in order:
        keep = [k for k in parts if not k & m]
        send = jnp.stack([parts[k ^ m] for k in keep], 0).astype(bf16)
        got = swap(send, "batch", m, nb)
        parts = {k: parts[k] + got[i].astype(f32) for i, k in enumerate(keep)}
    return parts[0]


def group_list(n, nt):
    bits = [1 << i for i in range(n.bit_length() - 1)]
    rest = [m for m in bits if m != nt]
    return [[nt]] + [rest[i : i + 2] for i in range(0, len(rest), 2)]


def members(group):
    found = [0]
    for m in group:
        found = found + [a ^ m for a in found]
    return found


def place(me, group):
    return sum(jnp.where((me & m) != 0, 1 << i, 0) for i, m in enumerate(group))


def all_sum(x, n, nt, me):
    done = []
    for group in group_list(n, nt):
        found = members(group)
        size = len(found)
        if x.shape[0] % (8 * size):
            terms = [x.astype(f32)] + [swap(x, AXES, m, n).astype(f32) for m in found[1:]]
            while len(terms) > 1:
                terms = [a + b for a, b in zip(terms[::2], terms[1::2])]
            x = terms[0].astype(bf16)
            continue
        h = x.shape[0] // size
        p = place(me, group)
        xs = x.reshape(size, h, x.shape[1])
        got = [
            swap(lax.dynamic_index_in_dim(xs, p ^ j, 0, False), AXES, found[j], n)
            for j in range(1, size)
        ]
        own = lax.dynamic_index_in_dim(xs, p, 0, False).astype(f32)
        x = sum((g.astype(f32) for g in got), own).astype(bf16)
        done.append((group, found, size, p))
    for group, found, size, p in reversed(done):
        out = jnp.zeros((size,) + x.shape, x.dtype)
        got = [x] + [swap(x, AXES, m, n) for m in found[1:]]
        for j in range(size):
            out = lax.dynamic_update_index_in_dim(out, got[j], p ^ j, 0)
        x = out.reshape(size * x.shape[0], x.shape[1])
    return x


def hot(ids, width, dtype):
    return (ids[:, None] == jnp.arange(width, dtype=jnp.int32)[None, :]).astype(dtype)


def encode(samples, animal_ids, w_in, bias_animal, w_out):
    one_hot = hot(animal_ids, bias_animal.shape[0], f32)
    pre_act = jnp.dot(samples, w_in, preferred_element_type=f32) + jnp.dot(
        one_hot, bias_animal, precision=lax.Precision.HIGHEST
    )
    hidden = jax.nn.gelu(pre_act).astype(bf16)
    latent = jnp.dot(hidden, w_out, preferred_element_type=f32)
    radius = jnp.sqrt(jnp.sum(latent * latent, axis=1, keepdims=True) + epsilon)
    return (pre_act, hidden, latent, radius, (latent / radius).astype(bf16))


def fetch_rows(recording, owner, row, nt, me_t):
    held = recording.shape[0]
    refs = row.shape[0]
    cap = min(refs, 2 * refs // nt)
    rows = jnp.dot(
        hot(jnp.where(owner == me_t, row, -1), held, bf16), recording, preferred_element_type=bf16
    )
    if cap < refs:
        owner_hot = hot(owner, nt, jnp.int32)
        slot = jnp.sum((jnp.cumsum(owner_hot, axis=0) - owner_hot) * owner_hot, axis=1)
    for k in range(1, nt):
        wanted = owner == (me_t ^ k)
        if cap < refs:
            pick = wanted[None, :] & (slot[None, :] == jnp.arange(cap, dtype=jnp.int32)[:, None])
            ask = jnp.max(jnp.where(pick, row[None, :], -1), axis=1)
        else:
            ask = jnp.where(wanted, row, -1)
        asked = swap(ask, "tm", k, nt)
        found = jnp.dot(hot(asked, held, bf16), recording, preferred_element_type=bf16)
        got = swap(found, "tm", k, nt)
        if cap < refs:
            got = jnp.dot(pick.T.astype(bf16), got, preferred_element_type=bf16)
        rows = rows + got
    return rows


def backward(animal_ids, enc, samples, grad_unit, w_out):
    pre_act, hidden, latent, radius, _ = enc
    inner = jnp.sum(latent * grad_unit, axis=1, keepdims=True)
    grad_latent = ((grad_unit - latent * inner / (radius * radius)) / radius).astype(bf16)
    grad_hidden = jnp.dot(grad_latent, w_out.T, preferred_element_type=f32)
    grad_pre = jax.vjp(jax.nn.gelu, pre_act)[1](grad_hidden)[0].astype(bf16)
    embed = w_out.shape[1]
    wide = jnp.concatenate([samples, hot(animal_ids, embed, bf16)], 1)
    top = lax.dot_general(wide, grad_pre, (((0,), (0,)), ((), ())), preferred_element_type=f32)
    low = lax.dot_general(grad_latent, hidden, (((0,), (0,)), ((), ())), preferred_element_type=f32)
    return jnp.concatenate([top, low], 0)


def on_device(
    ref_rows,
    neg_rows,
    recording,
    pos_owner,
    pos_row,
    ref_animal,
    neg_animal,
    w_in,
    bias_animal,
    w_out,
):
    refs = ref_rows.shape[0]
    channels = w_in.shape[0]
    embed = w_out.shape[1]
    animals = bias_animal.shape[0]
    nt = lax.axis_size("tm")
    nb = lax.axis_size("batch")
    n = nt * nb
    me_b = lax.axis_index("batch")
    me_t = lax.axis_index("tm")
    me = me_b * nt + me_t

    neg = encode(neg_rows, neg_animal, w_in, bias_animal, w_out)
    pos_rows = fetch_rows(recording, pos_owner[:, 0], pos_row, nt, me_t)
    pool = gather_batch(neg[4], nb, me_b)
    ref = encode(ref_rows, ref_animal, w_in, bias_animal, w_out)
    pos = encode(pos_rows, ref_animal, w_in, bias_animal, w_out)
    u, v = ref[4], pos[4]

    pos_score = jnp.sum(u.astype(f32) * v.astype(f32), axis=1) / logit_sharpness_divisor
    scores = (
        lax.dot_general(u, pool, (((1,), (1,)), ((), ())), preferred_element_type=f32)
        / logit_sharpness_divisor
    )
    exponent = jnp.exp(scores - shift_bound)
    pos_exp = jnp.exp(pos_score - shift_bound)
    normalizer = pos_exp + jnp.sum(exponent, axis=1)
    ref_loss = jnp.log(normalizer) + shift_bound - pos_score
    weights = (exponent / normalizer[:, None]).astype(bf16)
    pos_pull = (pos_exp / normalizer - 1.0)[:, None]
    scale = float(refs * n) ** (-0.5) / logit_sharpness_divisor
    share = scale * lax.dot_general(
        weights, u, (((0,), (0,)), ((), ())), preferred_element_type=f32
    )
    grad_neg = scatter_batch(share, nb, me_b)
    grad_ref = scale * (
        jnp.dot(weights, pool, preferred_element_type=f32) + pos_pull * v.astype(f32)
    )
    grad_pos = scale * pos_pull * u.astype(f32)

    both = tuple(jnp.concatenate([a, b], 0) for a, b in zip(ref, pos))
    total = backward(
        jnp.concatenate([ref_animal, ref_animal]),
        both,
        jnp.concatenate([ref_rows, pos_rows], 0),
        jnp.concatenate([grad_ref, grad_pos], 0),
        w_out,
    ) + backward(neg_animal, neg, neg_rows, grad_neg, w_out)
    total = all_sum(total.astype(bf16), n, nt, me)
    grad_w_in = total[:channels]
    grad_bias = total[channels : channels + animals].astype(f32)
    grad_w_out = total[channels + embed :].T.astype(f32)
    return (ref_loss, grad_w_in, grad_w_out, grad_bias)


def solution(mesh):
    in_specs = (
        P(("batch", "tm"), None),
        P(("batch", "tm"), None),
        P("tm", None),
        P(("batch", "tm"), None),
        P(("batch", "tm")),
        P(("batch", "tm")),
        P(("batch", "tm")),
        P(),
        P(),
        P(),
    )
    out_specs = (P(("batch", "tm")), P(), P(), P())
    return jax.shard_map(
        on_device, mesh=mesh, in_specs=in_specs, out_specs=out_specs, check_vma=False
    )
```

```python
import functools

import jax
import jax.numpy as jnp
from jax import lax
from jax.experimental import pallas as pl
from jax.experimental.pallas import tpu as pltpu
from jax.sharding import PartitionSpec as P

logit_sharpness_divisor = 0.1
shift_bound = 10.0
epsilon = 1e-06
AXES = ("batch", "tm")
bf16 = jnp.bfloat16
f32 = jnp.float32


def swap(x, axes, mask, n):
    return lax.ppermute(x, axes, [(i, i ^ mask) for i in range(n)])


def batch_masks(nb):
    return [1 << i for i in range(nb.bit_length() - 1)]


def gather_batch(x, nb, me):
    masks = batch_masks(nb)
    order = masks[2:][::-1] + masks[1:2] + masks[:1]
    rows = x.shape[0]
    parts = {0: x}
    for m in order:
        keys = list(parts)
        block = jnp.concatenate([parts[k] for k in keys], 0) if len(keys) > 1 else parts[keys[0]]
        got = swap(block, "batch", m, nb)
        for i, k in enumerate(keys):
            parts[k ^ m] = got[i * rows : (i + 1) * rows]
    out = jnp.zeros((nb,) + x.shape, x.dtype)
    for k, part in parts.items():
        out = lax.dynamic_update_index_in_dim(out, part, me ^ k, 0)
    return out.reshape((nb * rows,) + x.shape[1:])


def scatter_batch(x, nb, me, total):
    masks = batch_masks(nb)
    order = masks[:1] + masks[1:][::-1]
    xs = x.reshape((nb, x.shape[0] // nb) + x.shape[1:])
    parts = {k: lax.dynamic_index_in_dim(xs, me ^ k, 0, False) for k in range(nb)}
    for step, m in enumerate(order):
        keep = [k for k in parts if not k & m]
        send = jnp.stack([parts[k ^ m] for k in keep], 0).astype(bf16)
        if step == 2:
            send, total = lax.optimization_barrier((send, total))
        got = swap(send, "batch", m, nb)
        if len(keep) == 1:
            return parts[0], got[0], total
        parts = {k: parts[k] + got[i].astype(f32) for i, k in enumerate(keep)}


def group_list(n, nt):
    bits = [1 << i for i in range(n.bit_length() - 1)]
    rest = [m for m in bits if m != nt]
    return [[nt]] + [rest[i : i + 2] for i in range(0, len(rest), 2)]


def members(group):
    found = [0]
    for m in group:
        found = found + [a ^ m for a in found]
    return found


def place(me, group):
    return sum(jnp.where((me & m) != 0, 1 << i, 0) for i, m in enumerate(group))


def all_sum(x, n, nt, me):
    done = []
    for group in group_list(n, nt):
        found = members(group)
        size = len(found)
        if x.shape[0] % (8 * size):
            terms = [x.astype(f32)] + [swap(x, AXES, m, n).astype(f32) for m in found[1:]]
            while len(terms) > 1:
                terms = [a + b for a, b in zip(terms[::2], terms[1::2])]
            x = terms[0].astype(bf16)
            continue
        h = x.shape[0] // size
        p = place(me, group)
        xs = x.reshape(size, h, x.shape[1])
        got = [
            swap(lax.dynamic_index_in_dim(xs, p ^ j, 0, False), AXES, found[j], n)
            for j in range(1, size)
        ]
        own = lax.dynamic_index_in_dim(xs, p, 0, False).astype(f32)
        x = sum((g.astype(f32) for g in got), own).astype(bf16)
        done.append((group, found, size, p))
    for group, found, size, p in reversed(done[1:]):
        out = jnp.zeros((size,) + x.shape, x.dtype)
        got = [x] + [swap(x, AXES, m, n) for m in found[1:]]
        for j in range(size):
            out = lax.dynamic_update_index_in_dim(out, got[j], p ^ j, 0)
        x = out.reshape(size * x.shape[0], x.shape[1])
    return x, swap(x, AXES, nt, n)


def hot(ids, width, dtype):
    return (ids[:, None] == jnp.arange(width, dtype=jnp.int32)[None, :]).astype(dtype)


def nt_dot(a, b):
    return lax.dot_general(a, b, (((1,), (1,)), ((), ())), preferred_element_type=f32)


def tn_dot(a, b):
    return lax.dot_general(a, b, (((0,), (0,)), ((), ())), preferred_element_type=f32)


def hot_columns(ids, width):
    found = lax.broadcasted_iota(jnp.int32, (width, ids.shape[1]), 0) == ids
    return jnp.where(found, 1.0, 0.0).astype(bf16)


def gelu_pair(x):
    c = 0.7978845608028654
    square = x * x
    t = jnp.tanh(c * (x + 0.044715 * (square * x)))
    half = 0.5 * (1.0 + t)
    slope = half + (0.5 * x) * ((1.0 - t) * (1.0 + t)) * (c + (3.0 * 0.044715 * c) * square)
    return (x * half).astype(bf16), slope


def forward(rows, ids, w_in, bias, w_out):
    embed = w_out.shape[1]
    table = bias[...]
    table = jnp.concatenate([table, jnp.zeros((embed - table.shape[0], table.shape[1]), f32)], 0)
    one_hot = hot_columns(ids, embed)
    added = None
    for _ in range(3):
        piece = table.astype(bf16)
        table = table - piece.astype(f32)
        part = tn_dot(one_hot, piece)
        added = part if added is None else added + part
    pre = jnp.dot(rows, w_in[...], preferred_element_type=f32) + added
    latent = jnp.dot(gelu_pair(pre)[0], w_out[...], preferred_element_type=f32)
    radius = jnp.sqrt(jnp.sum(latent * latent, axis=1, keepdims=True) + epsilon)
    return pre, latent, (latent / radius).astype(bf16)


def front_kernel(count, me_ref, *refs):
    held, (u_ref, unit_ref, own_ref), scratch, sems = (
        refs[:count],
        refs[count : count + 3],
        refs[count + 3 : -1],
        refs[-1],
    )
    copies = [
        pltpu.make_async_copy(src, dst, sems.at[i]) for i, (src, dst) in enumerate(zip(held, scratch))
    ]
    for copy in copies:
        copy.start()
    w_in, bias, w_out, neg_ids, neg_rows, ref_ids, ref_rows, owner, row, recording = scratch
    for copy in copies[:5]:
        copy.wait()
    unit_ref[...] = forward(neg_rows[...], neg_ids[...], w_in, bias, w_out)[2]
    for copy in copies[5:7]:
        copy.wait()
    u_ref[...] = forward(ref_rows[...], ref_ids[...], w_in, bias, w_out)[2]
    for copy in copies[7:]:
        copy.wait()
    pick_kernel(me_ref, owner, row, recording, own_ref)


def score_kernel(
    scale, count, own, ids, u_ref, pool_ref, w_in, bias, w_out, *refs
):
    rows = own[...]
    for got in refs[:count]:
        rows = rows + got[...]
    rows_ref, share_ref, loss_ref, grad_ref, grad_pos = refs[count:]
    rows_ref[...] = rows
    v = forward(rows, ids[...], w_in, bias, w_out)[2]
    u, pool = u_ref[...], pool_ref[...]
    uf, vf = u.astype(f32), v.astype(f32)
    pos_score = jnp.sum(uf * vf, axis=1, keepdims=True) / logit_sharpness_divisor
    exponent = jnp.exp(nt_dot(u, pool) / logit_sharpness_divisor - shift_bound)
    pos_exp = jnp.exp(pos_score - shift_bound)
    normalizer = pos_exp + jnp.sum(exponent, axis=1, keepdims=True)
    weights = (exponent / normalizer).astype(bf16)
    share_ref[...] = scale * tn_dot(weights, u)
    loss = jnp.log(normalizer) + shift_bound - pos_score
    loss_ref[...] = jnp.broadcast_to(loss, uf.shape).T[:1]
    pull = pos_exp / normalizer - 1.0
    grad_ref[...] = scale * (jnp.dot(weights, pool, preferred_element_type=f32) + pull * vf)
    grad_pos[...] = scale * pull * uf


def share_of(rows, ids, grad_unit, w_in, bias, w_out):
    pre, latent, _ = forward(rows, ids, w_in, bias, w_out)
    w_out = w_out[...]
    power = jnp.sum(latent * latent, axis=1, keepdims=True) + epsilon
    radius = jnp.sqrt(power)
    inner = jnp.sum(latent * grad_unit, axis=1, keepdims=True)
    grad_latent = ((grad_unit - latent * (inner / (radius * radius))) / radius).astype(bf16)
    hidden, slope = gelu_pair(pre)
    grad_pre = (nt_dot(grad_latent, w_out) * slope).astype(bf16)
    bias = jnp.dot(hot_columns(ids, w_out.shape[1]), grad_pre, preferred_element_type=f32)
    return tn_dot(rows, grad_pre), tn_dot(grad_latent, hidden), bias


def parts_of(total, embed):
    half, small = total.shape[0] // 2 - embed, total.shape[0] // 2
    return half, slice(0, half), slice(half, small), slice(small, small + half), slice(small + half, None)


def two_sets_kernel(*refs):
    w_out, total = refs[-2], refs[-1]
    a = share_of(*(r[...] for r in refs[:3]), *refs[6:9])
    b = share_of(*(r[...] for r in refs[3:6]), *refs[6:9])
    big, low, bias = (x + y for x, y in zip(a, b))
    half, first, out, second, animals = parts_of(total, w_out.shape[1])
    total[first, :] = big[:half]
    total[out, :] = low
    total[second, :] = big[half:]
    total[animals, :] = bias


def add_set_kernel(rows, ids, kept, got, w_in, bias, w_out, before, total):
    grad_unit = kept[...] + got[...].astype(f32)
    big, low, bias = share_of(rows[...], ids[...], grad_unit, w_in, bias, w_out)
    half, first, out, second, animals = parts_of(total, w_out.shape[1])
    total[first, :] = (before[first, :] + big[:half]).astype(bf16)
    total[out, :] = (before[out, :] + low).astype(bf16)
    total[second, :] = (before[second, :] + big[half:]).astype(bf16)
    total[animals, :] = (before[animals, :] + bias).astype(bf16)


def finish_kernel(core_ref, own, other, grad_w_in, grad_w_out, grad_bias):
    half = grad_w_in.shape[0] // 2
    animals = grad_bias.shape[0]

    def put(first, second):
        grad_w_in[:half, :] = first[:half, :]
        grad_w_in[half:, :] = second[:half, :]
        grad_w_out[...] = first[half:, :].astype(f32).T
        grad_bias[...] = second[half : half + animals, :].astype(f32)

    @pl.when(core_ref[0] == 0)
    def _():
        put(own, other)

    @pl.when(core_ref[0] != 0)
    def _():
        put(other, own)


def call(kernel, name, out, *args, scalars=0, limit=12, space=pltpu.VMEM, scratch=()):
    whole = pl.BlockSpec(memory_space=pltpu.VMEM)
    given = pl.BlockSpec(memory_space=space)
    shapes = [jax.ShapeDtypeStruct(*o) for o in out]
    return pl.pallas_call(
        kernel,
        name=name,
        out_shape=shapes,
        in_specs=[pl.BlockSpec(memory_space=pltpu.SMEM)] * scalars + [given] * (len(args) - scalars),
        out_specs=[whole] * len(out),
        scratch_shapes=list(scratch),
        compiler_params=pltpu.CompilerParams(vmem_limit_bytes=limit * 2**20),
    )(*args)


def slots(owner, row, nt, me_t):
    refs = row.shape[0]
    cap = 2 * refs // nt
    owner_hot = hot(owner, nt, jnp.int32)
    slot = jnp.sum((jnp.cumsum(owner_hot, axis=0) - owner_hot) * owner_hot, axis=1)
    found = []
    for k in range(1, nt):
        wanted = owner == (me_t ^ k)
        pick = wanted[None, :] & (slot[None, :] == jnp.arange(cap, dtype=jnp.int32)[:, None])
        ask = jnp.max(jnp.where(pick, row[None, :], -1), axis=1)
        found.append((pick, jnp.where(ask < 0, -1, me_t ^ k)[None, :], ask[None, :]))
    return found


def pick_kernel(me_ref, owner, row, recording, rows):
    wanted = jnp.where(owner[...] == me_ref[0], row[...], -1)
    one_hot = hot_columns(wanted, recording.shape[0])
    rows[...] = tn_dot(one_hot, recording[...]).astype(bf16)


def pick_rows(me, owner, row, recording):
    out = [((row.shape[1], recording.shape[1]), bf16)]
    return call(pick_kernel, "pick", out, me, owner, row, recording, scalars=1)[0]


def on_device(
    ref_rows,
    neg_rows,
    recording,
    pos_owner,
    pos_row,
    ref_animal,
    neg_animal,
    w_in,
    bias_animal,
    w_out,
):
    refs = ref_rows.shape[0]
    channels = w_in.shape[0]
    embed = w_out.shape[1]
    animals = bias_animal.shape[0]
    nt = lax.axis_size("tm")
    nb = lax.axis_size("batch")
    n = nt * nb
    me_b = lax.axis_index("batch")
    me_t = lax.axis_index("tm")
    me = me_b * nt + me_t

    owner, row = pos_owner.reshape(1, refs), pos_row.reshape(1, refs)
    ref_ids, neg_ids = ref_animal[None, :], neg_animal[None, :]
    here = me_t.reshape(1)
    if nt == 2:
        asks = [(None, owner, row)]
    else:
        asks = slots(pos_owner[:, 0], pos_row, nt, me_t)
    asked = [(swap(o, "tm", k, nt), swap(r, "tm", k, nt)) for k, (_, o, r) in enumerate(asks, 1)]
    weights = (w_in, bias_animal, w_out)
    inputs = (*weights, neg_ids, neg_rows, ref_ids, ref_rows, owner, row, recording)
    inputs = [pltpu.with_memory_space_constraint(x, pltpu.HBM) for x in inputs]
    u, neg_unit, own = call(
        functools.partial(front_kernel, len(inputs)),
        "front",
        [
            ((refs, embed), bf16),
            ((neg_rows.shape[0], embed), bf16),
            ((refs, recording.shape[1]), bf16),
        ],
        here,
        *inputs,
        scalars=1,
        space=pltpu.HBM,
        scratch=[pltpu.VMEM(x.shape, x.dtype) for x in inputs]
        + [pltpu.SemaphoreType.DMA((len(inputs),))],
    )
    found = [pick_rows(here, o, r, recording) for o, r in asked]
    neg_unit, found = lax.optimization_barrier((neg_unit, found))
    got = [swap(f, "tm", k, nt) for k, f in enumerate(found, 1)]
    pool = gather_batch(neg_unit, nb, me_b)
    got = [
        g if pick is None else jnp.dot(pick.T.astype(bf16), g, preferred_element_type=bf16)
        for (pick, _, _), g in zip(asks, got)
    ]

    scale = float(refs * n) ** (-0.5) / logit_sharpness_divisor
    out = [(ref_rows.shape, bf16), ((pool.shape[0], embed), f32), ((1, refs), f32)]
    out += [(u.shape, f32), (u.shape, f32)]
    pos_rows, share, loss, grad_ref, grad_pos = call(
        functools.partial(score_kernel, scale, len(got)),
        "scores",
        out,
        own,
        ref_ids,
        u,
        pool,
        *weights,
        *got,
        limit=max(12, 20 * refs * pool.shape[0] >> 20),
    )
    total = call(
        two_sets_kernel,
        "backward",
        [((channels + 2 * embed, w_in.shape[1]), f32)],
        *(ref_rows, ref_ids, grad_ref),
        *(pos_rows, ref_ids, grad_pos),
        *weights,
    )[0]
    kept, last, total = scatter_batch(share, nb, me_b, total)
    total = call(
        add_set_kernel,
        "backward_neg",
        [(total.shape, bf16)],
        *(neg_rows, neg_ids, kept, last, *weights, total),
    )[0]
    own, other = all_sum(total, n, nt, me)
    grad_w_in, grad_w_out, grad_bias = call(
        finish_kernel,
        "finish",
        [(w_in.shape, bf16), (w_out.shape, f32), (bias_animal.shape, f32)],
        lax.rem(me_b, 2).reshape(1),
        own,
        other,
        scalars=1,
    )
    return (loss.reshape(refs), grad_w_in, grad_w_out, grad_bias)


def solution(mesh):
    in_specs = (
        P(("batch", "tm"), None),
        P(("batch", "tm"), None),
        P("tm", None),
        P(("batch", "tm"), None),
        P(("batch", "tm")),
        P(("batch", "tm")),
        P(("batch", "tm")),
        P(),
        P(),
        P(),
    )
    out_specs = (P(("batch", "tm")), P(), P(), P())
    return jax.shard_map(
        on_device, mesh=mesh, in_specs=in_specs, out_specs=out_specs, check_vma=False
    )
```

```python
import functools

import jax
import jax.numpy as jnp
from jax import lax
from jax.experimental import pallas as pl
from jax.experimental.pallas import tpu as pltpu
from jax.sharding import PartitionSpec as P

logit_sharpness_divisor = 0.1
shift_bound = 10.0
epsilon = 1e-06
AXES = ("batch", "tm")
bf16 = jnp.bfloat16
f32 = jnp.float32


def swap(x, axes, mask, n):
    return lax.ppermute(x, axes, [(i, i ^ mask) for i in range(n)])


def batch_masks(nb):
    return [1 << i for i in range(nb.bit_length() - 1)]


def gather_batch(x, nb, w, wide):
    masks = batch_masks(nb)
    order = masks[2:][::-1] + masks[1:2] + masks[:1]
    rows = x.shape[0]
    parts = {0: x}
    for m in order:
        keys = list(parts)
        block = jnp.concatenate([parts[k] for k in keys], 0) if len(keys) > 1 else parts[keys[0]]
        if m == masks[1]:
            block, wide = lax.optimization_barrier((block, wide))
        got = swap(block, "batch", m, nb)
        for i, k in enumerate(keys):
            parts[k ^ m] = got[i * rows : (i + 1) * rows]
    out = jnp.zeros((nb,) + x.shape, x.dtype)
    for k, part in parts.items():
        out = put(out, part, w["b", k])
    return out.reshape((nb * rows,) + x.shape[1:]), wide


def near_masks(nb):
    return batch_masks(nb)[1:3]


def spread(x, masks, nb):
    for m in masks:
        x = jnp.concatenate([x, swap(x, "batch", m, nb)], 0)
    return x


def kept_order(nb):
    masks = batch_masks(nb)
    high = [sum(m for i, m in enumerate(masks[3:]) if j >> i & 1) for j in range(nb >> 3)]
    return [h ^ k for h in high for k in members(near_masks(nb))]


def scatter_batch(kept, sent, nb, wide):
    masks = batch_masks(nb)
    x = kept + swap(sent, "batch", masks[0], nb).astype(f32)
    for m in masks[3:][::-1]:
        half = x.shape[0] // 2
        send, wide = lax.optimization_barrier((x[half:].astype(bf16), wide))
        x = x[:half] + swap(send, "batch", m, nb).astype(f32)
    return x, wide


def near_sum(x, m, nb, other):
    keep = members(near_masks(nb))
    send, other = lax.optimization_barrier((x.astype(bf16), other))
    got = swap(send, "batch", m, nb)
    rows = x.shape[0] // len(keep)
    at = [keep.index(k ^ m) * rows for k in keep]
    return x + jnp.concatenate([got[i : i + rows] for i in at], 0).astype(f32), other


def far_groups(nb, nt):
    rest = [1 << i for i in range(nt.bit_length() - 1)] + [m * nt for m in batch_masks(nb)[3:]]
    return [rest[i : i + 2] for i in range(0, len(rest), 2)]


def members(group):
    found = [0]
    for m in group:
        found = found + [a ^ m for a in found]
    return found


def place(me, group):
    return sum(jnp.where((me & m) != 0, 1 << i, 0) for i, m in enumerate(group))


def take(x, i):
    return lax.dynamic_index_in_dim(x, i, 0, False, allow_negative_indices=False)


def put(x, part, i):
    return lax.dynamic_update_index_in_dim(x, part, i, 0, allow_negative_indices=False)


def positions(nb, nt, me_b, me_t):
    me = me_b * nt + me_t
    near = [m * nt for m in near_masks(nb)]
    w = {("b", k): me_b ^ k for k in range(nb)}
    for group in [[nt], near] + far_groups(nb, nt):
        p = place(me, group)
        for j in range(1 << len(group)):
            w[tuple(group), j] = p ^ j
    w["at"] = w[(nt,), 0] * (1 << len(near)) + w[tuple(near), 0]
    return w


def split_pair(x, nb, nt, w):
    near = [m * nt for m in near_masks(nb)]
    n, found = nb * nt, members(near)
    halves = x.reshape(2, x.shape[0] // 2, x.shape[1])
    got = swap(take(halves, w[(nt,), 1]), AXES, nt, n)
    own = take(halves, w[(nt,), 0])
    x = (own.astype(f32) + got.astype(f32)).astype(bf16)
    xs = x.reshape(len(found), x.shape[0] // len(found), x.shape[1])
    return [take(xs, w[tuple(near), j]) for j in range(len(found))]


def split_near(pieces, nb, nt):
    found = members([m * nt for m in near_masks(nb)])
    return pieces[:1] + [swap(x, AXES, m, nb * nt) for x, m in zip(pieces[1:], found[1:])]


def join(x, group, w, n):
    found = members(group)
    out = jnp.zeros((len(found),) + x.shape, x.dtype)
    got = [x] + [swap(x, AXES, m, n) for m in found[1:]]
    for j, g in enumerate(got):
        out = put(out, g, w[tuple(group), j])
    return out.reshape(len(found) * x.shape[0], x.shape[1])


def finish_sum(x, nb, nt, w):
    n = nb * nt
    done = [[m * nt for m in near_masks(nb)]]
    for group in far_groups(nb, nt):
        found = members(group)
        size = len(found)
        if x.shape[0] % (8 * size):
            terms = [x.astype(f32)] + [swap(x, AXES, m, n).astype(f32) for m in found[1:]]
            while len(terms) > 1:
                terms = [a + b for a, b in zip(terms[::2], terms[1::2])]
            x = terms[0].astype(bf16)
            continue
        xs = x.reshape(size, x.shape[0] // size, x.shape[1])
        got = [
            swap(take(xs, w[tuple(group), j]), AXES, found[j], n)
            for j in range(1, size)
        ]
        own = take(xs, w[tuple(group), 0]).astype(f32)
        x = sum((g.astype(f32) for g in got), own).astype(bf16)
        done.append(group)
    for group in reversed(done):
        x = join(x, group, w, n)
    return x, swap(x, AXES, nt, n)


def hot(ids, width, dtype):
    return (ids[:, None] == jnp.arange(width, dtype=jnp.int32)[None, :]).astype(dtype)


def nt_dot(a, b):
    return lax.dot_general(a, b, (((1,), (1,)), ((), ())), preferred_element_type=f32)


def tn_dot(a, b, preferred_element_type=f32):
    return lax.dot_general(
        a, b, (((0,), (0,)), ((), ())), preferred_element_type=preferred_element_type
    )


def hot_columns(ids, width):
    found = lax.broadcasted_iota(jnp.int32, (width, ids.shape[1]), 0) == ids
    return jnp.where(found, 1.0, 0.0).astype(bf16)


def gelu_pair(x):
    c = 0.7978845608028654
    square = x * x
    t = jnp.tanh(c * (x + 0.044715 * (square * x)))
    half = 0.5 * (1.0 + t)
    slope = half + (0.5 * x) * ((1.0 - t) * (1.0 + t)) * (c + (3.0 * 0.044715 * c) * square)
    return (x * half).astype(bf16), slope


def forward(rows, one_hot, w_in, bias, w_out, dot=tn_dot):
    embed = w_out.shape[1]
    table = bias[...]
    table = jnp.concatenate([table, jnp.zeros((embed - table.shape[0], table.shape[1]), f32)], 0)
    added = None
    for _ in range(3):
        piece = table.astype(bf16)
        table = table - piece.astype(f32)
        part = dot(one_hot, piece, preferred_element_type=f32)
        added = part if added is None else added + part
    pre = jnp.dot(rows, w_in[...], preferred_element_type=f32) + added
    latent = jnp.dot(gelu_pair(pre)[0], w_out[...], preferred_element_type=f32)
    radius = jnp.sqrt(jnp.sum(latent * latent, axis=1, keepdims=True) + epsilon)
    return pre, latent, (latent / radius).astype(bf16)


def front_kernel(count, me_ref, *refs):
    held, (u_ref, unit_ref, own_ref, wide_ref), scratch, sems = (
        refs[:count],
        refs[count : count + 4],
        refs[count + 4 : -1],
        refs[-1],
    )
    copies = [
        pltpu.make_async_copy(src, dst, sems.at[i]) for i, (src, dst) in enumerate(zip(held, scratch))
    ]
    for copy in copies:
        copy.start()
    w_in, bias, w_out, neg_ids, neg_rows, ref_ids, ref_rows, owner, row, recording = scratch
    for copy in copies[:5]:
        copy.wait()
    embed, channels = w_out.shape[1], w_in.shape[0]
    one_hot = hot_columns(neg_ids[...], embed)
    unit_ref[...] = forward(neg_rows[...], one_hot, w_in, bias, w_out)[2]
    wide_ref[:, :channels] = neg_rows[...]
    wide_ref[:, channels:] = one_hot.astype(f32).T.astype(bf16)
    for copy in copies[5:7]:
        copy.wait()
    one_hot = hot_columns(ref_ids[...], embed)
    u_ref[...] = forward(ref_rows[...], one_hot, w_in, bias, w_out)[2]
    for copy in copies[7:]:
        copy.wait()
    pick_kernel(me_ref, owner, row, recording, own_ref)


def score_kernel(scale, count, order, me_ref, own, ids, u_ref, pool_ref, w_in, bias, w_out, *refs):
    rows = own[...]
    for got in refs[:count]:
        rows = rows + got[...]
    rows_ref, kept_ref, sent_ref, loss_ref, grad_ref, grad_pos, share_ref = refs[count:]
    rows_ref[...] = rows
    v = forward(rows, hot_columns(ids[...], w_out.shape[1]), w_in, bias, w_out)[2]
    u, pool = u_ref[...], pool_ref[...]
    uf, vf = u.astype(f32), v.astype(f32)
    pos_score = jnp.sum(uf * vf, axis=1, keepdims=True) / logit_sharpness_divisor
    exponent = jnp.exp(nt_dot(u, pool) / logit_sharpness_divisor - shift_bound)
    pos_exp = jnp.exp(pos_score - shift_bound)
    normalizer = pos_exp + jnp.sum(exponent, axis=1, keepdims=True)
    weights = (exponent / normalizer).astype(bf16)
    share_ref[...] = scale * tn_dot(weights, u)
    rows = kept_ref.shape[0] // len(order)
    for i, k in enumerate(order):
        at = pl.multiple_of((me_ref[0] ^ k) * rows, rows)
        kept_ref[i * rows : (i + 1) * rows, :] = share_ref[pl.ds(at, rows), :]
        at = pl.multiple_of((me_ref[0] ^ k ^ 1) * rows, rows)
        sent_ref[i * rows : (i + 1) * rows, :] = share_ref[pl.ds(at, rows), :].astype(bf16)
    loss = jnp.log(normalizer) + shift_bound - pos_score
    loss_ref[...] = jnp.broadcast_to(loss, uf.shape).T[:1]
    pull = pos_exp / normalizer - 1.0
    grad_ref[...] = scale * (jnp.dot(weights, pool, preferred_element_type=f32) + pull * vf)
    grad_pos[...] = scale * pull * uf


def pulled_back(rows, one_hot, grad_unit, w_in, bias, w_out, dot=tn_dot):
    pre, latent, _ = forward(rows, one_hot, w_in, bias, w_out, dot)
    power = jnp.sum(latent * latent, axis=1, keepdims=True) + epsilon
    radius = jnp.sqrt(power)
    inner = jnp.sum(latent * grad_unit, axis=1, keepdims=True)
    grad_latent = ((grad_unit - latent * (inner / (radius * radius))) / radius).astype(bf16)
    hidden, slope = gelu_pair(pre)
    return hidden, grad_latent, (nt_dot(grad_latent, w_out[...]) * slope).astype(bf16)


def piece_sizes(channels, embed, pieces):
    return channels // (2 * pieces), embed // pieces


def two_sets_kernel(pieces, a_rows, a_ids, a_grad, b_rows, b_ids, b_grad, w_in, bias, w_out, total):
    embed = w_out.shape[1]
    big, low, animal = 0.0, 0.0, 0.0
    for rows, ids, grad in ((a_rows, a_ids, a_grad), (b_rows, b_ids, b_grad)):
        one_hot = hot_columns(ids[...], embed)
        hidden, grad_latent, grad_pre = pulled_back(
            rows[...], one_hot, grad[...], w_in, bias, w_out
        )
        big = big + tn_dot(rows[...], grad_pre)
        low = low + tn_dot(grad_latent, hidden)
        animal = animal + jnp.dot(one_hot, grad_pre, preferred_element_type=f32)
    top, small = piece_sizes(w_in.shape[0], embed, pieces)
    for i in range(2 * pieces):
        at, q = i * (top + small), i % pieces
        below = low if i < pieces else animal
        total[at : at + top, :] = big[i * top : (i + 1) * top].astype(bf16)
        total[at + top : at + top + small, :] = below[q * small : (q + 1) * small].astype(bf16)


def near_kernel(pieces, at_ref, wide, mine, other, w_in, bias, w_out, *refs):
    terms, out, smalls = refs[:pieces], refs[pieces], refs[pieces + 1]
    channels, embed = w_in.shape[0], w_out.shape[1]
    grad_unit = jnp.concatenate([mine[...], other[...]], 0).astype(f32)
    one_hot = wide[:, channels:]
    hidden, grad_latent, grad_pre = pulled_back(
        wide[:, :channels], one_hot, grad_unit, w_in, bias, w_out, jnp.dot
    )
    top, small = piece_sizes(channels, embed, pieces)
    smalls[:embed, :] = tn_dot(grad_latent, hidden)
    smalls[embed:, :] = tn_dot(one_hot, grad_pre)
    at = at_ref[0]
    big = tn_dot(wide[:, pl.ds(pl.multiple_of(at * top, top), top)], grad_pre)
    low = smalls[pl.ds(pl.multiple_of(at * small, small), small), :]
    got = terms[0][...].astype(f32)
    for term in terms[1:]:
        got = got + term[...].astype(f32)
    out[:top, :] = (got[:top] + big).astype(bf16)
    out[top:, :] = (got[top:] + low).astype(bf16)


def finish_kernel(pieces, core_ref, own, other, grad_w_in, grad_w_out, grad_bias):
    half = grad_w_in.shape[0] // 2
    animals = grad_bias.shape[0]
    top, small = piece_sizes(2 * half, grad_w_out.shape[1], pieces)

    def put(first, second):
        lows = []
        for q in range(pieces):
            at = q * (top + small)
            grad_w_in[q * top : (q + 1) * top, :] = first[at : at + top, :]
            grad_w_in[half + q * top : half + (q + 1) * top, :] = second[at : at + top, :]
            lows.append(first[at + top : at + top + small, :])
        grad_w_out[...] = jnp.concatenate(lows, 0).astype(f32).T
        grad_bias[...] = second[top : top + animals, :].astype(f32)

    @pl.when(core_ref[0] == 0)
    def _():
        put(own, other)

    @pl.when(core_ref[0] != 0)
    def _():
        put(other, own)


def call(kernel, name, out, *args, scalars=0, limit=12, space=pltpu.VMEM, scratch=()):
    whole = pl.BlockSpec(memory_space=pltpu.VMEM)
    given = pl.BlockSpec(memory_space=space)
    shapes = [jax.ShapeDtypeStruct(*o) for o in out]
    return pl.pallas_call(
        kernel,
        name=name,
        out_shape=shapes,
        in_specs=[pl.BlockSpec(memory_space=pltpu.SMEM)] * scalars + [given] * (len(args) - scalars),
        out_specs=[whole] * len(out),
        scratch_shapes=list(scratch),
        compiler_params=pltpu.CompilerParams(vmem_limit_bytes=limit * 2**20),
    )(*args)


def slots(owner, row, nt, me_t):
    refs = row.shape[0]
    cap = 2 * refs // nt
    owner_hot = hot(owner, nt, jnp.int32)
    slot = jnp.sum((jnp.cumsum(owner_hot, axis=0) - owner_hot) * owner_hot, axis=1)
    found = []
    for k in range(1, nt):
        wanted = owner == (me_t ^ k)
        pick = wanted[None, :] & (slot[None, :] == jnp.arange(cap, dtype=jnp.int32)[:, None])
        ask = jnp.max(jnp.where(pick, row[None, :], -1), axis=1)
        found.append((pick, jnp.where(ask < 0, -1, me_t ^ k)[None, :], ask[None, :]))
    return found


def pick_kernel(me_ref, owner, row, recording, rows):
    wanted = jnp.where(owner[...] == me_ref[0], row[...], -1)
    one_hot = hot_columns(wanted, recording.shape[0])
    rows[...] = tn_dot(one_hot, recording[...]).astype(bf16)


def pick_rows(me, owner, row, recording):
    out = [((row.shape[1], recording.shape[1]), bf16)]
    return call(pick_kernel, "pick", out, me, owner, row, recording, scalars=1)[0]


def on_device(
    ref_rows,
    neg_rows,
    recording,
    pos_owner,
    pos_row,
    ref_animal,
    neg_animal,
    w_in,
    bias_animal,
    w_out,
):
    refs = ref_rows.shape[0]
    channels = w_in.shape[0]
    embed = w_out.shape[1]
    animals = bias_animal.shape[0]
    nt = lax.axis_size("tm")
    nb = lax.axis_size("batch")
    n = nt * nb
    me_b = lax.axis_index("batch")
    me_t = lax.axis_index("tm")
    w = positions(nb, nt, me_b, me_t)
    here, *found = lax.optimization_barrier((me_t.reshape(1), *w.values()))
    w = dict(zip(w, found))

    owner, row = pos_owner.reshape(1, refs), pos_row.reshape(1, refs)
    ref_ids, neg_ids = ref_animal[None, :], neg_animal[None, :]
    if nt == 2:
        asks = [(None, owner, row)]
    else:
        asks = slots(pos_owner[:, 0], pos_row, nt, me_t)
    asked = [(swap(o, "tm", k, nt), swap(r, "tm", k, nt)) for k, (_, o, r) in enumerate(asks, 1)]
    weights = (w_in, bias_animal, w_out)
    inputs = (*weights, neg_ids, neg_rows, ref_ids, ref_rows, owner, row, recording)
    inputs = [pltpu.with_memory_space_constraint(x, pltpu.HBM) for x in inputs]
    u, neg_unit, own, wide = call(
        functools.partial(front_kernel, len(inputs)),
        "front",
        [
            ((refs, embed), bf16),
            ((neg_rows.shape[0], embed), bf16),
            ((refs, recording.shape[1]), bf16),
            ((neg_rows.shape[0], channels + embed), bf16),
        ],
        here,
        *inputs,
        scalars=1,
        space=pltpu.HBM,
        scratch=[pltpu.VMEM(x.shape, x.dtype) for x in inputs]
        + [pltpu.SemaphoreType.DMA((len(inputs),))],
    )
    found = [pick_rows(here, o, r, recording) for o, r in asked]
    neg_unit, found = lax.optimization_barrier((neg_unit, found))
    got = [swap(f, "tm", k, nt) for k, f in enumerate(found, 1)]
    near = near_masks(nb)
    wide = spread(wide, near[:1], nb)
    pool, wide = gather_batch(neg_unit, nb, w, wide)
    wide = spread(wide, near[1:], nb)
    got = [
        g if pick is None else jnp.dot(pick.T.astype(bf16), g, preferred_element_type=bf16)
        for (pick, _, _), g in zip(asks, got)
    ]

    scale = float(refs * n) ** (-0.5) / logit_sharpness_divisor
    half = pool.shape[0] // 2
    out = [(ref_rows.shape, bf16), ((half, embed), f32), ((half, embed), bf16), ((1, refs), f32)]
    out += [(u.shape, f32), (u.shape, f32)]
    pos_rows, kept, sent, loss, grad_ref, grad_pos = call(
        functools.partial(score_kernel, scale, len(got), kept_order(nb)),
        "scores",
        out,
        w["b", 0].reshape(1),
        own,
        ref_ids,
        u,
        pool,
        *weights,
        *got,
        scalars=1,
        limit=max(12, 20 * refs * pool.shape[0] >> 20),
        scratch=[pltpu.VMEM((pool.shape[0], embed), f32)],
    )
    pieces = 1 << len(near)
    columns = w_in.shape[1]
    total = call(
        functools.partial(two_sets_kernel, pieces),
        "backward",
        [((channels + 2 * embed, columns), bf16)],
        *(ref_rows, ref_ids, grad_ref),
        *(pos_rows, ref_ids, grad_pos),
        *weights,
    )[0]
    mine, wide = scatter_batch(kept, sent, nb, wide)
    mine, total = near_sum(mine, near[0], nb, total)
    parts = split_pair(total, nb, nt, w)
    mine, parts = near_sum(mine, near[1], nb, parts)
    terms = split_near(parts, nb, nt)
    wide = spread(wide, [1], nb)
    mine = mine.astype(bf16)
    other = swap(mine, "batch", 1, nb)
    total = call(
        functools.partial(near_kernel, pieces),
        "backward_near",
        [(terms[0].shape, bf16)],
        w["at"].reshape(1),
        *(wide, mine, other, *weights, *terms),
        scalars=1,
        scratch=[pltpu.VMEM((2 * embed, columns), f32)],
    )[0]
    own, other = finish_sum(total, nb, nt, w)
    grad_w_in, grad_w_out, grad_bias = call(
        functools.partial(finish_kernel, pieces),
        "finish",
        [(w_in.shape, bf16), (w_out.shape, f32), (bias_animal.shape, f32)],
        w[(nt,), 0].reshape(1),
        own,
        other,
        scalars=1,
    )
    return (loss.reshape(refs), grad_w_in, grad_w_out, grad_bias)


def solution(mesh):
    in_specs = (
        P(("batch", "tm"), None),
        P(("batch", "tm"), None),
        P("tm", None),
        P(("batch", "tm"), None),
        P(("batch", "tm")),
        P(("batch", "tm")),
        P(("batch", "tm")),
        P(),
        P(),
        P(),
    )
    out_specs = (P(("batch", "tm")), P(), P(), P())
    return jax.shard_map(
        on_device, mesh=mesh, in_specs=in_specs, out_specs=out_specs, check_vma=False
    )
```

```python
import functools

import jax
import jax.numpy as jnp
from jax import lax
from jax.experimental import pallas as pl
from jax.experimental.pallas import tpu as pltpu
from jax.sharding import PartitionSpec as P

logit_sharpness_divisor = 0.1
shift_bound = 10.0
epsilon = 1e-06
AXES = ("batch", "tm")
bf16 = jnp.bfloat16
f32 = jnp.float32


def swap(x, axes, mask, n):
    return lax.ppermute(x, axes, [(i, i ^ mask) for i in range(n)])


def batch_masks(nb):
    return [1 << i for i in range(nb.bit_length() - 1)]


def gather_batch(x, nb, w, wide, later):
    masks = batch_masks(nb)
    order = masks[2:][::-1] + masks[1:2] + masks[:1]
    rows = x.shape[0]
    parts = {0: x}
    for m in order:
        keys = list(parts)
        block = jnp.concatenate([parts[k] for k in keys], 0) if len(keys) > 1 else parts[keys[0]]
        if len(keys) == 2:
            block, later = lax.optimization_barrier((block, later))
        if m == masks[1]:
            block, wide = lax.optimization_barrier((block, wide))
        got = swap(block, "batch", m, nb)
        for i, k in enumerate(keys):
            parts[k ^ m] = got[i * rows : (i + 1) * rows]
    out = jnp.zeros((nb,) + x.shape, x.dtype)
    for k, part in parts.items():
        out = put(out, part, w["b", k])
    return out.reshape((nb * rows,) + x.shape[1:]), wide, later


def near_masks(nb):
    return batch_masks(nb)[1:3]


def spread(x, masks, nb):
    for m in masks:
        x = jnp.concatenate([x, swap(x, "batch", m, nb)], 0)
    return x


def kept_order(nb):
    masks = batch_masks(nb)
    high = [sum(m for i, m in enumerate(masks[3:]) if j >> i & 1) for j in range(nb >> 3)]
    return [h ^ k for h in high for k in members(near_masks(nb))]


def scatter_batch(kept, sent, nb, wide):
    masks = batch_masks(nb)
    x = kept + swap(sent, "batch", masks[0], nb).astype(f32)
    for m in masks[3:][::-1]:
        half = x.shape[0] // 2
        send, wide = lax.optimization_barrier((x[half:].astype(bf16), wide))
        x = x[:half] + swap(send, "batch", m, nb).astype(f32)
    return x, wide


def near_sum(x, m, nb, other):
    keep = members(near_masks(nb))
    send, other = lax.optimization_barrier((x.astype(bf16), other))
    got = swap(send, "batch", m, nb)
    rows = x.shape[0] // len(keep)
    at = [keep.index(k ^ m) * rows for k in keep]
    return x + jnp.concatenate([got[i : i + rows] for i in at], 0).astype(f32), other


def far_groups(nb, nt):
    rest = [1 << i for i in range(nt.bit_length() - 1)] + [m * nt for m in batch_masks(nb)[3:]]
    return [rest[i : i + 2] for i in range(0, len(rest), 2)]


def members(group):
    found = [0]
    for m in group:
        found = found + [a ^ m for a in found]
    return found


def place(me, group):
    return sum(jnp.where((me & m) != 0, 1 << i, 0) for i, m in enumerate(group))


def take(x, i):
    return lax.dynamic_index_in_dim(x, i, 0, False, allow_negative_indices=False)


def put(x, part, i):
    return lax.dynamic_update_index_in_dim(x, part, i, 0, allow_negative_indices=False)


def positions(nb, nt, me_b, me_t):
    me = me_b * nt + me_t
    near = [m * nt for m in near_masks(nb)]
    w = {("b", k): me_b ^ k for k in range(nb)}
    for group in [[nt], near] + far_groups(nb, nt):
        p = place(me, group)
        for j in range(1 << len(group)):
            w[tuple(group), j] = p ^ j
    w["at"] = w[(nt,), 0] * (1 << len(near)) + w[tuple(near), 0]
    return w


def split_pair(x, nb, nt, w):
    near = [m * nt for m in near_masks(nb)]
    n, found = nb * nt, members(near)
    halves = x.reshape(2, x.shape[0] // 2, x.shape[1])
    got = swap(take(halves, w[(nt,), 1]), AXES, nt, n)
    own = take(halves, w[(nt,), 0])
    x = (own.astype(f32) + got.astype(f32)).astype(bf16)
    xs = x.reshape(len(found), x.shape[0] // len(found), x.shape[1])
    return [take(xs, w[tuple(near), j]) for j in range(len(found))]


def split_near(pieces, nb, nt):
    found = members([m * nt for m in near_masks(nb)])
    return pieces[:1] + [swap(x, AXES, m, nb * nt) for x, m in zip(pieces[1:], found[1:])]


def join(x, group, w, n):
    found = members(group)
    out = jnp.zeros((len(found),) + x.shape, x.dtype)
    got = [x] + [swap(x, AXES, m, n) for m in found[1:]]
    for j, g in enumerate(got):
        out = put(out, g, w[tuple(group), j])
    return out.reshape(len(found) * x.shape[0], x.shape[1])


def finish_sum(x, nb, nt, w):
    n = nb * nt
    done = []
    for group in far_groups(nb, nt):
        found = members(group)
        size = len(found)
        if x.shape[0] % (8 * size):
            terms = [x.astype(f32)] + [swap(x, AXES, m, n).astype(f32) for m in found[1:]]
            while len(terms) > 1:
                terms = [a + b for a, b in zip(terms[::2], terms[1::2])]
            x = terms[0].astype(bf16)
            continue
        xs = x.reshape(size, x.shape[0] // size, x.shape[1])
        got = [
            swap(take(xs, w[tuple(group), j]), AXES, found[j], n)
            for j in range(1, size)
        ]
        own = take(xs, w[tuple(group), 0]).astype(f32)
        x = sum((g.astype(f32) for g in got), own).astype(bf16)
        done.append(group)
    for group in reversed(done):
        x = join(x, group, w, n)
    found = members([m * nt for m in near_masks(nb)])
    own = [x] + [swap(x, AXES, m, n) for m in found[1:]]
    return own, [swap(x, AXES, nt, n) for x in own]


def hot(ids, width, dtype):
    return (ids[:, None] == jnp.arange(width, dtype=jnp.int32)[None, :]).astype(dtype)


def nt_dot(a, b):
    return lax.dot_general(a, b, (((1,), (1,)), ((), ())), preferred_element_type=f32)


def tn_dot(a, b, preferred_element_type=f32):
    return lax.dot_general(
        a, b, (((0,), (0,)), ((), ())), preferred_element_type=preferred_element_type
    )


def hot_columns(ids, width):
    found = lax.broadcasted_iota(jnp.int32, (width, ids.shape[1]), 0) == ids
    return jnp.where(found, 1.0, 0.0).astype(bf16)


def gelu_pair(x):
    c = 0.7978845608028654
    square = x * x
    t = jnp.tanh(c * (x + 0.044715 * (square * x)))
    half = 0.5 * (1.0 + t)
    slope = half + (0.5 * x) * ((1.0 - t) * (1.0 + t)) * (c + (3.0 * 0.044715 * c) * square)
    return (x * half).astype(bf16), slope


def forward(rows, one_hot, w_in, bias, w_out, dot=tn_dot):
    embed = w_out.shape[1]
    table = bias[...]
    table = jnp.concatenate([table, jnp.zeros((embed - table.shape[0], table.shape[1]), f32)], 0)
    added = None
    for _ in range(3):
        piece = table.astype(bf16)
        table = table - piece.astype(f32)
        part = dot(one_hot, piece, preferred_element_type=f32)
        added = part if added is None else added + part
    pre = jnp.dot(rows, w_in[...], preferred_element_type=f32) + added
    hidden, slope = gelu_pair(pre)
    latent = jnp.dot(hidden, w_out[...], preferred_element_type=f32)
    radius = jnp.sqrt(jnp.sum(latent * latent, axis=1, keepdims=True) + epsilon)
    return (latent / radius).astype(bf16), latent, hidden, slope, pre


def front_kernel(count, *refs):
    held, (unit_ref, wide_ref), scratch, sems = (
        refs[:count],
        refs[count : count + 2],
        refs[count + 2 : -1],
        refs[-1],
    )
    copies = [
        pltpu.make_async_copy(src, dst, sems.at[i]) for i, (src, dst) in enumerate(zip(held, scratch))
    ]
    for copy in copies:
        copy.start()
    w_in, bias, w_out, ids, rows = scratch
    for copy in copies:
        copy.wait()
    embed, channels = w_out.shape[1], w_in.shape[0]
    one_hot = hot_columns(ids[...], embed)
    unit_ref[...] = forward(rows[...], one_hot, w_in, bias, w_out)[0]
    wide_ref[:, :channels] = rows[...]
    wide_ref[:, channels:] = one_hot.astype(f32).T.astype(bf16)


def refs_kernel(rows, ids, w_in, bias, w_out, unit, latent, hidden, slope):
    values = forward(rows[...], hot_columns(ids[...], w_out.shape[1]), w_in, bias, w_out)
    for out, value in zip((unit, latent, hidden, slope), values):
        out[...] = value


def near_forward_kernel(wide, w_in, bias, w_out, latent, hidden, slope):
    channels = w_in.shape[0]
    values = forward(wide[:, :channels], wide[:, channels:], w_in, bias, w_out, jnp.dot)
    for out, value in zip((latent, hidden, slope), values[1:]):
        out[...] = value


def score_kernel(
    scale, count, order, me_ref, here_ref, owner, own, ids, u_ref, pool_ref, w_in, bias, w_out, *refs
):
    held = jnp.where(owner[...] == here_ref[0], 1.0, 0.0)
    held = jnp.broadcast_to(held, (w_out.shape[1], held.shape[1])).T[:, :1] > 0.5
    rows = refs[0][...]
    for got in refs[1:count]:
        rows = rows + got[...]
    rows = jnp.where(held, own[...].astype(f32), rows.astype(f32)).astype(bf16)
    rows_ref, latent_ref, pre_ref, kept_ref, sent_ref, loss_ref, grad_ref, grad_pos = refs[count:-1]
    share_ref = refs[-1]
    rows_ref[...] = rows
    values = forward(rows, hot_columns(ids[...], w_out.shape[1]), w_in, bias, w_out)
    v = values[0]
    latent_ref[...], pre_ref[...] = values[1], values[4]
    u, pool = u_ref[...], pool_ref[...]
    uf, vf = u.astype(f32), v.astype(f32)
    pos_score = jnp.sum(uf * vf, axis=1, keepdims=True) / logit_sharpness_divisor
    exponent = jnp.exp(nt_dot(u, pool) / logit_sharpness_divisor - shift_bound)
    pos_exp = jnp.exp(pos_score - shift_bound)
    normalizer = pos_exp + jnp.sum(exponent, axis=1, keepdims=True)
    weights = (exponent / normalizer).astype(bf16)
    share_ref[...] = scale * tn_dot(weights, u)
    rows = kept_ref.shape[0] // len(order)
    for i, k in enumerate(order):
        at = pl.multiple_of((me_ref[0] ^ k) * rows, rows)
        kept_ref[i * rows : (i + 1) * rows, :] = share_ref[pl.ds(at, rows), :]
        at = pl.multiple_of((me_ref[0] ^ k ^ 1) * rows, rows)
        sent_ref[i * rows : (i + 1) * rows, :] = share_ref[pl.ds(at, rows), :].astype(bf16)
    loss = jnp.log(normalizer) + shift_bound - pos_score
    loss_ref[...] = jnp.broadcast_to(loss, uf.shape).T[:1]
    pull = pos_exp / normalizer - 1.0
    grad_ref[...] = scale * (jnp.dot(weights, pool, preferred_element_type=f32) + pull * vf)
    grad_pos[...] = scale * pull * uf


def pulled_back(latent, slope, grad_unit, w_out):
    power = jnp.sum(latent * latent, axis=1, keepdims=True) + epsilon
    radius = jnp.sqrt(power)
    inner = jnp.sum(latent * grad_unit, axis=1, keepdims=True)
    grad_latent = ((grad_unit - latent * (inner / (radius * radius))) / radius).astype(bf16)
    return grad_latent, (nt_dot(grad_latent, w_out[...]) * slope).astype(bf16)


def piece_sizes(channels, embed, pieces):
    return channels // (2 * pieces), embed // pieces


def two_sets_kernel(
    pieces, ids, a_rows, a_latent, a_hidden, a_slope, a_grad, b_rows, b_latent, b_pre, b_grad, w_out, total
):
    embed, channels = w_out.shape[1], a_rows.shape[1]
    one_hot = hot_columns(ids[...], embed)
    a_latent_grad, a_pre_grad = pulled_back(a_latent[...], a_slope[...], a_grad[...], w_out)
    b_hidden, b_slope = gelu_pair(b_pre[...])
    b_latent_grad, b_pre_grad = pulled_back(b_latent[...], b_slope, b_grad[...], w_out)
    big = tn_dot(a_rows[...], a_pre_grad) + tn_dot(b_rows[...], b_pre_grad)
    low = tn_dot(a_latent_grad, a_hidden[...]) + tn_dot(b_latent_grad, b_hidden)
    animal = jnp.dot(one_hot, a_pre_grad, preferred_element_type=f32)
    animal = animal + jnp.dot(one_hot, b_pre_grad, preferred_element_type=f32)
    top, small = piece_sizes(channels, embed, pieces)
    for i in range(2 * pieces):
        at, q = i * (top + small), i % pieces
        below = low if i < pieces else animal
        total[at : at + top, :] = big[i * top : (i + 1) * top].astype(bf16)
        total[at + top : at + top + small, :] = below[q * small : (q + 1) * small].astype(bf16)


def near_kernel(pieces, at_ref, wide, latent, hidden, slope, mine, other, w_out, *refs):
    terms, out, smalls = refs[:pieces], refs[pieces], refs[pieces + 1]
    embed = w_out.shape[1]
    channels = wide.shape[1] - embed
    grad_unit = jnp.concatenate([mine[...], other[...]], 0).astype(f32)
    one_hot = wide[:, channels:]
    grad_latent, grad_pre = pulled_back(latent[...], slope[...], grad_unit, w_out)
    top, small = piece_sizes(channels, embed, pieces)
    smalls[:embed, :] = tn_dot(grad_latent, hidden[...])
    smalls[embed:, :] = tn_dot(one_hot, grad_pre)
    at = at_ref[0]
    big = tn_dot(wide[:, pl.ds(pl.multiple_of(at * top, top), top)], grad_pre)
    low = smalls[pl.ds(pl.multiple_of(at * small, small), small), :]
    got = terms[0][...].astype(f32)
    for term in terms[1:]:
        got = got + term[...].astype(f32)
    out[:top, :] = (got[:top] + big).astype(bf16)
    out[top:, :] = (got[top:] + low).astype(bf16)


def finish_kernel(pieces, core_ref, *refs):
    places, own, other = (refs[i * pieces : (i + 1) * pieces] for i in range(3))
    grad_w_in, grad_w_out, grad_bias, lows = refs[3 * pieces :]
    embed = grad_w_out.shape[1]
    top, small = piece_sizes(grad_w_in.shape[0], embed, pieces)
    for half, held in ((core_ref[0], own), (1 - core_ref[0], other)):
        for place_ref, piece in zip(places, held):
            at = half * pieces + place_ref[0]
            grad_w_in[pl.ds(pl.multiple_of(at * top, top), top), :] = piece[:top, :]
            lows[pl.ds(pl.multiple_of(at * small, small), small), :] = piece[top:, :].astype(f32)
    grad_w_out[...] = lows[:embed, :].T
    grad_bias[...] = lows[embed : embed + grad_bias.shape[0], :]


def call(kernel, name, out, *args, scalars=0, limit=12, space=pltpu.VMEM, scratch=()):
    whole = pl.BlockSpec(memory_space=pltpu.VMEM)
    given = pl.BlockSpec(memory_space=space)
    shapes = [jax.ShapeDtypeStruct(*o) for o in out]
    return pl.pallas_call(
        kernel,
        name=name,
        out_shape=shapes,
        in_specs=[pl.BlockSpec(memory_space=pltpu.SMEM)] * scalars + [given] * (len(args) - scalars),
        out_specs=[whole] * len(out),
        scratch_shapes=list(scratch),
        compiler_params=pltpu.CompilerParams(vmem_limit_bytes=limit * 2**20),
    )(*args)


def sets(rows, embed, width):
    return [((rows, embed), f32), ((rows, width), bf16), ((rows, width), f32)]


def slots(owner, row, nt, me_t):
    refs = row.shape[0]
    cap = 2 * refs // nt
    owner_hot = hot(owner, nt, jnp.int32)
    slot = jnp.sum((jnp.cumsum(owner_hot, axis=0) - owner_hot) * owner_hot, axis=1)
    found = []
    for k in range(1, nt):
        wanted = owner == (me_t ^ k)
        pick = wanted[None, :] & (slot[None, :] == jnp.arange(cap, dtype=jnp.int32)[:, None])
        found.append((pick, jnp.max(jnp.where(pick, row[None, :], -1), axis=1)[None, :]))
    return found


def pick_kernel(row, recording, rows):
    one_hot = hot_columns(row[...], recording.shape[0])
    rows[...] = tn_dot(one_hot, recording[...]).astype(bf16)


def pick_rows(row, recording):
    out = [((row.shape[1], recording.shape[1]), bf16)]
    return call(pick_kernel, "pick", out, row, recording)[0]


def on_device(
    ref_rows,
    neg_rows,
    recording,
    pos_owner,
    pos_row,
    ref_animal,
    neg_animal,
    w_in,
    bias_animal,
    w_out,
):
    refs = ref_rows.shape[0]
    channels = w_in.shape[0]
    embed = w_out.shape[1]
    animals = bias_animal.shape[0]
    nt = lax.axis_size("tm")
    nb = lax.axis_size("batch")
    n = nt * nb
    me_b = lax.axis_index("batch")
    me_t = lax.axis_index("tm")
    w = positions(nb, nt, me_b, me_t)
    here, *found = lax.optimization_barrier((me_t.reshape(1), *w.values()))
    w = dict(zip(w, found))

    owner, row = pos_owner.reshape(1, refs), pos_row.reshape(1, refs)
    ref_ids, neg_ids = ref_animal[None, :], neg_animal[None, :]
    if nt == 2:
        asks = [(None, row)]
    else:
        asks = slots(pos_owner[:, 0], pos_row, nt, me_t)
    asked = [swap(ask, "tm", k, nt) for k, (_, ask) in enumerate(asks, 1)]
    weights = (w_in, bias_animal, w_out)
    hidden_width = w_in.shape[1]
    inputs = (*weights, neg_ids, neg_rows)
    inputs = [pltpu.with_memory_space_constraint(x, pltpu.HBM) for x in inputs]
    negs = neg_rows.shape[0]
    here, *inputs = lax.optimization_barrier((here, *inputs))
    neg_unit, wide = call(
        functools.partial(front_kernel, len(inputs)),
        "front",
        [((negs, embed), bf16), ((negs, channels + embed), bf16)],
        *inputs,
        space=pltpu.HBM,
        scratch=[pltpu.VMEM(x.shape, x.dtype) for x in inputs]
        + [pltpu.SemaphoreType.DMA((len(inputs),))],
    )
    found = [pick_rows(ask, recording) for ask in asked]
    neg_unit, found, wide = lax.optimization_barrier((neg_unit, found, wide))
    got = [swap(f, "tm", k, nt) for k, f in enumerate(found, 1)]
    near = near_masks(nb)
    wide = spread(wide, near[:1], nb)
    pool, wide, (ref_rows, row) = gather_batch(neg_unit, nb, w, wide, (ref_rows, row))
    wide = spread(wide, near[1:], nb)
    u, ref_latent, ref_hidden, ref_slope = call(
        refs_kernel,
        "refs",
        [((refs, embed), bf16), *sets(refs, embed, hidden_width)],
        *(ref_rows, ref_ids, *weights),
    )
    own = pick_rows(row, recording)
    got = [
        g if pick is None else jnp.dot(pick.T.astype(bf16), g, preferred_element_type=bf16)
        for (pick, _), g in zip(asks, got)
    ]

    scale = float(refs * n) ** (-0.5) / logit_sharpness_divisor
    half = pool.shape[0] // 2
    out = [(ref_rows.shape, bf16), (u.shape, f32), ((refs, hidden_width), f32)]
    out += [((half, embed), f32), ((half, embed), bf16), ((1, refs), f32)]
    out += [(u.shape, f32), (u.shape, f32)]
    pos_rows, pos_latent, pos_pre, kept, sent, loss, grad_ref, grad_pos = call(
        functools.partial(score_kernel, scale, len(got), kept_order(nb)),
        "scores",
        out,
        w["b", 0].reshape(1),
        here,
        owner,
        own,
        ref_ids,
        u,
        pool,
        *weights,
        *got,
        scalars=2,
        limit=max(12, 20 * refs * pool.shape[0] >> 20),
        scratch=[pltpu.VMEM((pool.shape[0], embed), f32)],
    )
    pieces = 1 << len(near)
    total = call(
        functools.partial(two_sets_kernel, pieces),
        "backward",
        [((channels + 2 * embed, hidden_width), bf16)],
        ref_ids,
        *(ref_rows, ref_latent, ref_hidden, ref_slope, grad_ref),
        *(pos_rows, pos_latent, pos_pre, grad_pos),
        w_out,
    )[0]
    mine, wide = scatter_batch(kept, sent, nb, wide)
    wide = spread(wide, [1], nb)
    parts = split_pair(total, nb, nt, w)
    mine, (parts, wide) = near_sum(mine, near[0], nb, (parts, wide))
    near_values = call(
        near_forward_kernel,
        "near_forward",
        sets(wide.shape[0], embed, hidden_width),
        *(wide, *weights),
    )
    terms = split_near(parts, nb, nt)
    mine, near_values = near_sum(mine, near[1], nb, near_values)
    mine = mine.astype(bf16)
    other = swap(mine, "batch", 1, nb)
    total = call(
        functools.partial(near_kernel, pieces),
        "backward_near",
        [(terms[0].shape, bf16)],
        w["at"].reshape(1),
        *(wide, *near_values, mine, other, w_out, *terms),
        scalars=1,
        scratch=[pltpu.VMEM((2 * embed, hidden_width), f32)],
    )[0]
    own, other = finish_sum(total, nb, nt, w)
    places = [w[tuple(m * nt for m in near), j].reshape(1) for j in range(pieces)]
    grad_w_in, grad_w_out, grad_bias = call(
        functools.partial(finish_kernel, pieces),
        "finish",
        [(w_in.shape, bf16), (w_out.shape, f32), (bias_animal.shape, f32)],
        w[(nt,), 0].reshape(1),
        *(*places, *own, *other),
        scalars=1 + pieces,
        scratch=[pltpu.VMEM((2 * embed, hidden_width), f32)],
    )
    return (loss.reshape(refs), grad_w_in, grad_w_out, grad_bias)


def solution(mesh):
    in_specs = (
        P(("batch", "tm"), None),
        P(("batch", "tm"), None),
        P("tm", None),
        P(("batch", "tm"), None),
        P(("batch", "tm")),
        P(("batch", "tm")),
        P(("batch", "tm")),
        P(),
        P(),
        P(),
    )
    out_specs = (P(("batch", "tm")), P(), P(), P())
    return jax.shard_map(
        on_device, mesh=mesh, in_specs=in_specs, out_specs=out_specs, check_vma=False
    )
```

```python
import functools

import jax
import jax.numpy as jnp
from jax import lax
from jax.experimental import pallas as pl
from jax.experimental.pallas import tpu as pltpu
from jax.sharding import PartitionSpec as P

logit_sharpness_divisor = 0.1
shift_bound = 10.0
epsilon = 1e-06
AXES = ("batch", "tm")
bf16 = jnp.bfloat16
f32 = jnp.float32


def swap(x, axes, mask, n):
    return lax.ppermute(x, axes, [(i, i ^ mask) for i in range(n)])


def batch_masks(nb):
    return [1 << i for i in range(nb.bit_length() - 1)]


def gather_batch(x, nb, w, wide, later):
    masks = batch_masks(nb)
    order = masks[2:][::-1] + masks[1:2] + masks[:1]
    rows = x.shape[0]
    parts = {0: x}
    for m in order:
        keys = list(parts)
        block = jnp.concatenate([parts[k] for k in keys], 0) if len(keys) > 1 else parts[keys[0]]
        if len(keys) == 2:
            block, later = lax.optimization_barrier((block, later))
        if m == masks[1]:
            block, wide = lax.optimization_barrier((block, wide))
        got = swap(block, "batch", m, nb)
        for i, k in enumerate(keys):
            parts[k ^ m] = got[i * rows : (i + 1) * rows]
    out = jnp.zeros((nb,) + x.shape, x.dtype)
    for k, part in parts.items():
        out = put(out, part, w["b", k])
    return out.reshape((nb * rows,) + x.shape[1:]), wide, later


def near_masks(nb):
    return batch_masks(nb)[1:3]


def spread(x, masks, nb):
    for m in masks:
        x = jnp.concatenate([x, swap(x, "batch", m, nb)], 0)
    return x


def kept_order(nb):
    masks = batch_masks(nb)
    high = [sum(m for i, m in enumerate(masks[3:]) if j >> i & 1) for j in range(nb >> 3)]
    return [h ^ k for h in high for k in members(near_masks(nb))]


def scatter_batch(kept, sent, nb, wide):
    masks = batch_masks(nb)
    x = kept + swap(sent, "batch", masks[0], nb).astype(f32)
    for m in masks[3:][::-1]:
        half = x.shape[0] // 2
        send, wide = lax.optimization_barrier((x[half:].astype(bf16), wide))
        x = x[:half] + swap(send, "batch", m, nb).astype(f32)
    return x, wide


def near_sum(x, m, nb, other):
    keep = members(near_masks(nb))
    send, other = lax.optimization_barrier((x.astype(bf16), other))
    got = swap(send, "batch", m, nb)
    rows = x.shape[0] // len(keep)
    at = [keep.index(k ^ m) * rows for k in keep]
    return x + jnp.concatenate([got[i : i + rows] for i in at], 0).astype(f32), other


def far_groups(nb, nt):
    rest = [1 << i for i in range(nt.bit_length() - 1)] + [m * nt for m in batch_masks(nb)[3:]]
    return [rest[i : i + 2] for i in range(0, len(rest), 2)]


def members(group):
    found = [0]
    for m in group:
        found = found + [a ^ m for a in found]
    return found


def place(me, group):
    return sum(jnp.where((me & m) != 0, 1 << i, 0) for i, m in enumerate(group))


def take(x, i):
    return lax.dynamic_index_in_dim(x, i, 0, False, allow_negative_indices=False)


def put(x, part, i):
    return lax.dynamic_update_index_in_dim(x, part, i, 0, allow_negative_indices=False)


def positions(nb, nt, me_b, me_t):
    me = me_b * nt + me_t
    near = [m * nt for m in near_masks(nb)]
    w = {("b", k): me_b ^ k for k in range(nb)}
    for group in [[nt], near] + far_groups(nb, nt):
        p = place(me, group)
        for j in range(1 << len(group)):
            w[tuple(group), j] = p ^ j
    w["at"] = w[(nt,), 0] * (1 << len(near)) + w[tuple(near), 0]
    return w


def split_pair(x, nb, nt, w):
    near = [m * nt for m in near_masks(nb)]
    n, found = nb * nt, members(near)
    halves = x.reshape(2, x.shape[0] // 2, x.shape[1])
    got = swap(take(halves, w[(nt,), 1]), AXES, nt, n)
    own = take(halves, w[(nt,), 0])
    x = (own.astype(f32) + got.astype(f32)).astype(bf16)
    xs = x.reshape(len(found), x.shape[0] // len(found), x.shape[1])
    return [take(xs, w[tuple(near), j]) for j in range(len(found))]


def split_near(pieces, nb, nt):
    found = members([m * nt for m in near_masks(nb)])
    return pieces[:1] + [swap(x, AXES, m, nb * nt) for x, m in zip(pieces[1:], found[1:])]


def join(x, group, w, n):
    found = members(group)
    out = jnp.zeros((len(found),) + x.shape, x.dtype)
    got = [x] + [swap(x, AXES, m, n) for m in found[1:]]
    for j, g in enumerate(got):
        out = put(out, g, w[tuple(group), j])
    return out


def finish_sum(x, nb, nt, w):
    n = nb * nt
    done = []
    for group in far_groups(nb, nt):
        found = members(group)
        size = len(found)
        if x.ndim == 2 or x.shape[0] != size:
            terms = [x.astype(f32)] + [swap(x, AXES, m, n).astype(f32) for m in found[1:]]
            while len(terms) > 1:
                terms = [a + b for a, b in zip(terms[::2], terms[1::2])]
            x = terms[0].astype(bf16)
            continue
        got = [swap(take(x, w[tuple(group), j]), AXES, found[j], n) for j in range(1, size)]
        own = take(x, w[tuple(group), 0]).astype(f32)
        x = sum((g.astype(f32) for g in got), own).astype(bf16)
        done.append(group)
    for group in reversed(done):
        x = join(x, group, w, n)
    found = members([m * nt for m in near_masks(nb)])
    own = [x] + [swap(x, AXES, m, n) for m in found[:0:-1]][::-1]
    return own, [swap(x, AXES, nt, n) for x in own]


def hot(ids, width, dtype):
    return (ids[:, None] == jnp.arange(width, dtype=jnp.int32)[None, :]).astype(dtype)


def nt_dot(a, b):
    return lax.dot_general(a, b, (((1,), (1,)), ((), ())), preferred_element_type=f32)


def tn_dot(a, b, preferred_element_type=f32):
    return lax.dot_general(
        a, b, (((0,), (0,)), ((), ())), preferred_element_type=preferred_element_type
    )


def hot_columns(ids, width):
    found = lax.broadcasted_iota(jnp.int32, (width, ids.shape[1]), 0) == ids
    return jnp.where(found, 1.0, 0.0).astype(bf16)


def gelu_pair(x):
    c = 0.7978845608028654
    square = x * x
    t = jnp.tanh(c * (x + 0.044715 * (square * x)))
    half = 0.5 * (1.0 + t)
    slope = half + (0.5 * x) * ((1.0 - t) * (1.0 + t)) * (c + (3.0 * 0.044715 * c) * square)
    return (x * half).astype(bf16), slope


def forward(rows, one_hot, w_in, bias, w_out, dot=tn_dot):
    embed = w_out.shape[1]
    table = bias[...]
    table = jnp.concatenate([table, jnp.zeros((embed - table.shape[0], table.shape[1]), f32)], 0)
    added = None
    for _ in range(3):
        piece = table.astype(bf16)
        table = table - piece.astype(f32)
        part = dot(one_hot, piece, preferred_element_type=f32)
        added = part if added is None else added + part
    pre = jnp.dot(rows, w_in[...], preferred_element_type=f32) + added
    hidden, slope = gelu_pair(pre)
    latent = jnp.dot(hidden, w_out[...], preferred_element_type=f32)
    radius = jnp.sqrt(jnp.sum(latent * latent, axis=1, keepdims=True) + epsilon)
    return (latent / radius).astype(bf16), latent, hidden, slope, pre


def front_kernel(count, *refs):
    held, (unit_ref, wide_ref), scratch, sems = (
        refs[:count],
        refs[count : count + 2],
        refs[count + 2 : -1],
        refs[-1],
    )
    copies = [
        pltpu.make_async_copy(src, dst, sems.at[i]) for i, (src, dst) in enumerate(zip(held, scratch))
    ]
    for copy in copies:
        copy.start()
    w_in, bias, w_out, ids, rows = scratch
    for copy in copies:
        copy.wait()
    embed, channels = w_out.shape[1], w_in.shape[0]
    one_hot = hot_columns(ids[...], embed)
    unit_ref[...] = forward(rows[...], one_hot, w_in, bias, w_out)[0]
    wide_ref[:, :channels] = rows[...]
    wide_ref[:, channels:] = one_hot.astype(f32).T.astype(bf16)


def refs_kernel(rows, ids, w_in, bias, w_out, unit, latent, hidden, slope):
    values = forward(rows[...], hot_columns(ids[...], w_out.shape[1]), w_in, bias, w_out)
    for out, value in zip((unit, latent, hidden, slope), values):
        out[...] = value


def near_forward_kernel(wide, w_in, bias, w_out, latent, hidden, slope):
    channels = w_in.shape[0]
    values = forward(wide[:, :channels], wide[:, channels:], w_in, bias, w_out, jnp.dot)
    for out, value in zip((latent, hidden, slope), values[1:]):
        out[...] = value


def exponent_kernel(u_ref, pool_ref, exponent_ref):
    scores = nt_dot(u_ref[...], pool_ref[...]) / logit_sharpness_divisor
    exponent_ref[...] = jnp.exp(scores - shift_bound)


def positives_kernel(here_ref, owner, own, ids, w_in, bias, w_out, *refs):
    gots, (rows_ref, unit_ref, latent_ref, pre_ref) = refs[:-4], refs[-4:]
    held = jnp.where(owner[...] == here_ref[0], 1.0, 0.0)
    held = jnp.broadcast_to(held, (w_out.shape[1], held.shape[1])).T[:, :1] > 0.5
    rows = gots[0][...]
    for got in gots[1:]:
        rows = rows + got[...]
    rows = jnp.where(held, own[...].astype(f32), rows.astype(f32)).astype(bf16)
    rows_ref[...] = rows
    values = forward(rows, hot_columns(ids[...], w_out.shape[1]), w_in, bias, w_out)
    unit_ref[...], latent_ref[...], pre_ref[...] = values[0], values[1], values[4]


def score_kernel(scale, order, me_ref, u_ref, v_ref, pool_ref, exponent_ref, *refs):
    kept_ref, sent_ref, loss_ref, grad_ref, grad_pos, share_ref = refs
    v = v_ref[...]
    u, pool = u_ref[...], pool_ref[...]
    uf, vf = u.astype(f32), v.astype(f32)
    pos_score = jnp.sum(uf * vf, axis=1, keepdims=True) / logit_sharpness_divisor
    exponent = exponent_ref[...]
    pos_exp = jnp.exp(pos_score - shift_bound)
    normalizer = pos_exp + jnp.sum(exponent, axis=1, keepdims=True)
    weights = (exponent / normalizer).astype(bf16)
    share_ref[...] = scale * tn_dot(weights, u)
    rows = kept_ref.shape[0] // len(order)
    for i, k in enumerate(order):
        at = pl.multiple_of((me_ref[0] ^ k) * rows, rows)
        kept_ref[i * rows : (i + 1) * rows, :] = share_ref[pl.ds(at, rows), :]
        at = pl.multiple_of((me_ref[0] ^ k ^ 1) * rows, rows)
        sent_ref[i * rows : (i + 1) * rows, :] = share_ref[pl.ds(at, rows), :].astype(bf16)
    loss = jnp.log(normalizer) + shift_bound - pos_score
    loss_ref[...] = jnp.broadcast_to(loss, uf.shape).T[:1]
    pull = pos_exp / normalizer - 1.0
    grad_ref[...] = scale * (jnp.dot(weights, pool, preferred_element_type=f32) + pull * vf)
    grad_pos[...] = scale * pull * uf


def pulled_back(latent, slope, grad_unit, w_out):
    power = jnp.sum(latent * latent, axis=1, keepdims=True) + epsilon
    radius = jnp.sqrt(power)
    inner = jnp.sum(latent * grad_unit, axis=1, keepdims=True)
    grad_latent = ((grad_unit - latent * (inner / (radius * radius))) / radius).astype(bf16)
    return grad_latent, (nt_dot(grad_latent, w_out[...]) * slope).astype(bf16)


def piece_sizes(channels, embed, animals, pieces):
    return channels // (2 * pieces), embed // (2 * pieces), -(-animals // 8) * 8


def two_sets_kernel(
    pieces, animals, ids, a_rows, a_latent, a_hidden, a_slope, a_grad, b_rows, b_latent, b_pre, b_grad, w_out, total
):
    embed, channels = w_out.shape[1], a_rows.shape[1]
    one_hot = hot_columns(ids[...], embed)
    a_latent_grad, a_pre_grad = pulled_back(a_latent[...], a_slope[...], a_grad[...], w_out)
    b_hidden, b_slope = gelu_pair(b_pre[...])
    b_latent_grad, b_pre_grad = pulled_back(b_latent[...], b_slope, b_grad[...], w_out)
    big = tn_dot(a_rows[...], a_pre_grad) + tn_dot(b_rows[...], b_pre_grad)
    low = tn_dot(a_latent_grad, a_hidden[...]) + tn_dot(b_latent_grad, b_hidden)
    animal = jnp.dot(one_hot, a_pre_grad, preferred_element_type=f32)
    animal = animal + jnp.dot(one_hot, b_pre_grad, preferred_element_type=f32)
    top, small, biases = piece_sizes(channels, embed, animals, pieces)
    for i in range(2 * pieces):
        at = i * (top + small + biases)
        total[at : at + top, :] = big[i * top : (i + 1) * top].astype(bf16)
        total[at + top : at + top + small, :] = low[i * small : (i + 1) * small].astype(bf16)
        total[at + top + small : at + top + small + biases, :] = animal[:biases].astype(bf16)


def near_kernel(pieces, animals, at_ref, wide, latent, hidden, slope, mine, other, w_out, *refs):
    terms, out, smalls = refs[:pieces], refs[pieces], refs[pieces + 1]
    embed = w_out.shape[1]
    channels = wide.shape[1] - embed
    grad_unit = jnp.concatenate([mine[...], other[...]], 0).astype(f32)
    one_hot = wide[:, channels:]
    grad_latent, grad_pre = pulled_back(latent[...], slope[...], grad_unit, w_out)
    top, small, biases = piece_sizes(channels, embed, animals, pieces)
    smalls[...] = tn_dot(grad_latent, hidden[...])
    at = at_ref[0]
    big = tn_dot(wide[:, pl.ds(pl.multiple_of(at * top, top), top)], grad_pre)
    low = smalls[pl.ds(pl.multiple_of(at * small, small), small), :]
    got = terms[0][...].astype(f32)
    for term in terms[1:]:
        got = got + term[...].astype(f32)
    got = got + jnp.concatenate([big, low, tn_dot(one_hot, grad_pre)[:biases]], 0)
    blocks, _, width = out.shape
    for i in range(blocks):
        out[i] = got[:, i * width : (i + 1) * width].astype(bf16)


def finish_kernel(pieces, core_ref, *refs):
    places, own, other = (refs[i * pieces : (i + 1) * pieces] for i in range(3))
    grad_w_in, grad_w_out, grad_bias, lows, bias_rows = refs[3 * pieces :]
    animals = grad_bias.shape[0]
    top, small, biases = piece_sizes(grad_w_in.shape[0], grad_w_out.shape[1], animals, pieces)
    blocks, _, width = own[0].shape
    for half, held in ((core_ref[0], own), (1 - core_ref[0], other)):
        for place_ref, piece in zip(places, held):
            at = half * pieces + place_ref[0]
            tops = pl.ds(pl.multiple_of(at * top, top), top)
            rows = pl.ds(pl.multiple_of(at * small, small), small)
            last = pl.ds(pl.multiple_of(at * biases, biases), biases)
            for i in range(blocks):
                columns = slice(i * width, (i + 1) * width)
                grad_w_in[tops, columns] = piece[i, :top, :]
                lows[rows, columns] = piece[i, top : top + small, :].astype(f32)
                bias_rows[last, columns] = piece[i, top + small :, :].astype(f32)
    grad_w_out[...] = lows[...].T
    grad_bias[...] = bias_rows[:animals, :]


def call(kernel, name, out, *args, scalars=0, limit=12, space=pltpu.VMEM, scratch=()):
    whole = pl.BlockSpec(memory_space=pltpu.VMEM)
    given = pl.BlockSpec(memory_space=space)
    shapes = [jax.ShapeDtypeStruct(*o) for o in out]
    return pl.pallas_call(
        kernel,
        name=name,
        out_shape=shapes,
        in_specs=[pl.BlockSpec(memory_space=pltpu.SMEM)] * scalars + [given] * (len(args) - scalars),
        out_specs=[whole] * len(out),
        scratch_shapes=list(scratch),
        compiler_params=pltpu.CompilerParams(vmem_limit_bytes=limit * 2**20),
    )(*args)


def sets(rows, embed, width):
    return [((rows, embed), f32), ((rows, width), bf16), ((rows, width), f32)]


def slots(owner, row, nt, me_t):
    refs = row.shape[0]
    cap = 2 * refs // nt
    owner_hot = hot(owner, nt, jnp.int32)
    slot = jnp.sum((jnp.cumsum(owner_hot, axis=0) - owner_hot) * owner_hot, axis=1)
    found = []
    for k in range(1, nt):
        wanted = owner == (me_t ^ k)
        pick = wanted[None, :] & (slot[None, :] == jnp.arange(cap, dtype=jnp.int32)[:, None])
        found.append((pick, jnp.max(jnp.where(pick, row[None, :], -1), axis=1)[None, :]))
    return found


def pick_kernel(row, recording, rows):
    one_hot = hot_columns(row[...], recording.shape[0])
    rows[...] = tn_dot(one_hot, recording[...]).astype(bf16)


def pick_rows(row, recording):
    out = [((row.shape[1], recording.shape[1]), bf16)]
    return call(pick_kernel, "pick", out, row, recording)[0]


def on_device(
    ref_rows,
    neg_rows,
    recording,
    pos_owner,
    pos_row,
    ref_animal,
    neg_animal,
    w_in,
    bias_animal,
    w_out,
):
    refs = ref_rows.shape[0]
    channels = w_in.shape[0]
    embed = w_out.shape[1]
    animals = bias_animal.shape[0]
    nt = lax.axis_size("tm")
    nb = lax.axis_size("batch")
    n = nt * nb
    me_b = lax.axis_index("batch")
    me_t = lax.axis_index("tm")
    w = positions(nb, nt, me_b, me_t)
    here, *found = lax.optimization_barrier((me_t.reshape(1), *w.values()))
    w = dict(zip(w, found))

    owner, row = pos_owner.reshape(1, refs), pos_row.reshape(1, refs)
    ref_ids, neg_ids = ref_animal[None, :], neg_animal[None, :]
    if nt == 2:
        asks = [(None, row)]
    else:
        asks = slots(pos_owner[:, 0], pos_row, nt, me_t)
    asked = [swap(ask, "tm", k, nt) for k, (_, ask) in enumerate(asks, 1)]
    weights = (w_in, bias_animal, w_out)
    hidden_width = w_in.shape[1]
    inputs = (*weights, neg_ids, neg_rows)
    inputs = [pltpu.with_memory_space_constraint(x, pltpu.HBM) for x in inputs]
    negs = neg_rows.shape[0]
    here, *inputs = lax.optimization_barrier((here, *inputs))
    neg_unit, wide = call(
        functools.partial(front_kernel, len(inputs)),
        "front",
        [((negs, embed), bf16), ((negs, channels + embed), bf16)],
        *inputs,
        space=pltpu.HBM,
        scratch=[pltpu.VMEM(x.shape, x.dtype) for x in inputs]
        + [pltpu.SemaphoreType.DMA((len(inputs),))],
    )
    found = [pick_rows(ask, recording) for ask in asked]
    neg_unit, found, wide = lax.optimization_barrier((neg_unit, found, wide))
    got = [swap(f, "tm", k, nt) for k, f in enumerate(found, 1)]
    near = near_masks(nb)
    wide = spread(wide, near[:1], nb)
    pool, wide, (ref_rows, row) = gather_batch(neg_unit, nb, w, wide, (ref_rows, row))
    wide = spread(wide, near[1:], nb)
    u, ref_latent, ref_hidden, ref_slope = call(
        refs_kernel,
        "refs",
        [((refs, embed), bf16), *sets(refs, embed, hidden_width)],
        *(ref_rows, ref_ids, *weights),
    )
    own = pick_rows(row, recording)
    got = [
        g if pick is None else jnp.dot(pick.T.astype(bf16), g, preferred_element_type=bf16)
        for (pick, _), g in zip(asks, got)
    ]

    scale = float(refs * n) ** (-0.5) / logit_sharpness_divisor
    exponent = call(
        exponent_kernel,
        "exponents",
        [((refs, pool.shape[0]), f32)],
        *(u, pool),
        limit=max(12, 12 * refs * pool.shape[0] >> 20),
    )[0]
    pos_rows, v, pos_latent, pos_pre = call(
        positives_kernel,
        "positives",
        [(ref_rows.shape, bf16), (u.shape, bf16), (u.shape, f32), ((refs, hidden_width), f32)],
        *(here, owner, own, ref_ids, *weights, *got),
        scalars=1,
    )
    half = pool.shape[0] // 2
    out = [((half, embed), f32), ((half, embed), bf16), ((1, refs), f32)]
    out += [(u.shape, f32), (u.shape, f32)]
    kept, sent, loss, grad_ref, grad_pos = call(
        functools.partial(score_kernel, scale, kept_order(nb)),
        "scores",
        out,
        *(w["b", 0].reshape(1), u, v, pool, exponent),
        scalars=1,
        limit=max(12, 20 * refs * pool.shape[0] >> 20),
        scratch=[pltpu.VMEM((pool.shape[0], embed), f32)],
    )
    pieces = 1 << len(near)
    piece_rows = sum(piece_sizes(channels, embed, animals, pieces))
    total = call(
        functools.partial(two_sets_kernel, pieces, animals),
        "backward",
        [((2 * pieces * piece_rows, hidden_width), bf16)],
        ref_ids,
        *(ref_rows, ref_latent, ref_hidden, ref_slope, grad_ref),
        *(pos_rows, pos_latent, pos_pre, grad_pos),
        w_out,
    )[0]
    mine, wide = scatter_batch(kept, sent, nb, wide)
    wide = spread(wide, [1], nb)
    parts = split_pair(total, nb, nt, w)
    mine, (parts, wide) = near_sum(mine, near[0], nb, (parts, wide))
    near_values = call(
        near_forward_kernel,
        "near_forward",
        sets(wide.shape[0], embed, hidden_width),
        *(wide, *weights),
    )
    terms = split_near(parts, nb, nt)
    mine, near_values = near_sum(mine, near[1], nb, near_values)
    mine = mine.astype(bf16)
    other = swap(mine, "batch", 1, nb)
    total = call(
        functools.partial(near_kernel, pieces, animals),
        "backward_near",
        [((hidden_width // 128, piece_rows, 128), bf16)],
        w["at"].reshape(1),
        *(wide, *near_values, mine, other, w_out, *terms),
        scalars=1,
        scratch=[pltpu.VMEM((embed, hidden_width), f32)],
    )[0]
    own, other = finish_sum(total, nb, nt, w)
    places = [w[tuple(m * nt for m in near), j].reshape(1) for j in range(pieces)]
    grad_w_in, grad_w_out, grad_bias = call(
        functools.partial(finish_kernel, pieces),
        "finish",
        [(w_in.shape, bf16), (w_out.shape, f32), (bias_animal.shape, f32)],
        w[(nt,), 0].reshape(1),
        *(*places, *own, *other),
        scalars=1 + pieces,
        scratch=[
            pltpu.VMEM((embed, hidden_width), f32),
            pltpu.VMEM((2 * pieces * piece_sizes(channels, embed, animals, pieces)[2], hidden_width), f32),
        ],
    )
    return (loss.reshape(refs), grad_w_in, grad_w_out, grad_bias)


def solution(mesh):
    in_specs = (
        P(("batch", "tm"), None),
        P(("batch", "tm"), None),
        P("tm", None),
        P(("batch", "tm"), None),
        P(("batch", "tm")),
        P(("batch", "tm")),
        P(("batch", "tm")),
        P(),
        P(),
        P(),
    )
    out_specs = (P(("batch", "tm")), P(), P(), P())
    return jax.shard_map(
        on_device, mesh=mesh, in_specs=in_specs, out_specs=out_specs, check_vma=False
    )
```

```python
import functools

import jax
import jax.numpy as jnp
from jax import lax
from jax.experimental import pallas as pl
from jax.experimental.pallas import tpu as pltpu
from jax.sharding import PartitionSpec as P

logit_sharpness_divisor = 0.1
shift_bound = 10.0
epsilon = 1e-06
AXES = ("batch", "tm")
bf16 = jnp.bfloat16
f32 = jnp.float32


def swap(x, axes, mask, n):
    return lax.ppermute(x, axes, [(i, i ^ mask) for i in range(n)])


def batch_masks(nb):
    return [1 << i for i in range(nb.bit_length() - 1)]


def gather_batch(x, nb, w, wide, later):
    masks = batch_masks(nb)
    order = masks[-1:] + masks[1:-2][::-1] + masks[-2:-1] + masks[:1]
    rows = x.shape[0]
    parts = {0: x}
    for m in order:
        keys = list(parts)
        block = jnp.concatenate([parts[k] for k in keys], 0) if len(keys) > 1 else parts[keys[0]]
        if len(keys) == 2:
            block, later = lax.optimization_barrier((block, later))
        if m == masks[-2]:
            block, wide = lax.optimization_barrier((block, wide))
        got = swap(block, "batch", m, nb)
        for i, k in enumerate(keys):
            parts[k ^ m] = got[i * rows : (i + 1) * rows]
    out = jnp.zeros((nb,) + x.shape, x.dtype)
    for k, part in parts.items():
        out = put(out, part, w["b", k])
    return out.reshape((nb * rows,) + x.shape[1:]), wide, later


def near_masks(nb):
    return batch_masks(nb)[1:3]


def spread(x, masks, nb):
    for m in masks:
        x = jnp.concatenate([x, swap(x, "batch", m, nb)], 0)
    return x


def wide_masks(nb):
    return batch_masks(nb)[:-3:-1]


def kept_order(nb):
    masks = batch_masks(nb)[1:-2]
    high = [sum(m for i, m in enumerate(masks) if j >> i & 1) for j in range(1 << len(masks))]
    return [h ^ k for h in high for k in members(wide_masks(nb))]


def scatter_batch(kept, sent, nb):
    masks = batch_masks(nb)
    x = kept + swap(sent, "batch", masks[0], nb).astype(f32)
    for m in masks[1:-2][::-1]:
        half = x.shape[0] // 2
        x = x[:half] + swap(x[half:].astype(bf16), "batch", m, nb).astype(f32)
    return x


def far_groups(nb, nt):
    rest = [1 << i for i in range(nt.bit_length() - 1)] + [m * nt for m in batch_masks(nb)[3:]]
    return [rest[i : i + 2] for i in range(0, len(rest), 2)]


def members(group):
    found = [0]
    for m in group:
        found = found + [a ^ m for a in found]
    return found


def place(me, group):
    return sum(jnp.where((me & m) != 0, 1 << i, 0) for i, m in enumerate(group))


def take(x, i):
    return lax.dynamic_index_in_dim(x, i, 0, False, allow_negative_indices=False)


def put(x, part, i):
    return lax.dynamic_update_index_in_dim(x, part, i, 0, allow_negative_indices=False)


def positions(nb, nt, me_b, me_t):
    me = me_b * nt + me_t
    near = [m * nt for m in near_masks(nb)]
    w = {("b", k): me_b ^ k for k in range(nb)}
    for group in [[nt], near] + far_groups(nb, nt):
        p = place(me, group)
        for j in range(1 << len(group)):
            w[tuple(group), j] = p ^ j
    return w


def split_pair(x, nb, nt, w):
    near = [m * nt for m in near_masks(nb)]
    n, found = nb * nt, members(near)
    halves = x.reshape(2, x.shape[0] // 2, x.shape[1])
    got = swap(take(halves, w[(nt,), 1]), AXES, nt, n)
    own = take(halves, w[(nt,), 0])
    x = (own.astype(f32) + got.astype(f32)).astype(bf16)
    xs = x.reshape(len(found), x.shape[0] // len(found), x.shape[1])
    return [take(xs, w[tuple(near), j]) for j in range(len(found))]


def split_near(pieces, nb, nt):
    found = members([m * nt for m in near_masks(nb)])
    return pieces[:1] + [swap(x, AXES, m, nb * nt) for x, m in zip(pieces[1:], found[1:])]


def join(x, group, w, n):
    found = members(group)
    out = jnp.zeros((len(found),) + x.shape, x.dtype)
    got = [x] + [swap(x, AXES, m, n) for m in found[1:]]
    for j, g in enumerate(got):
        out = put(out, g, w[tuple(group), j])
    return out


def finish_sum(x, nb, nt, w):
    n = nb * nt
    done = []
    for group in far_groups(nb, nt):
        found = members(group)
        size = len(found)
        if x.ndim == 2 or x.shape[0] != size:
            terms = [x.astype(f32)] + [swap(x, AXES, m, n).astype(f32) for m in found[1:]]
            while len(terms) > 1:
                terms = [a + b for a, b in zip(terms[::2], terms[1::2])]
            x = terms[0].astype(bf16)
            continue
        got = [swap(take(x, w[tuple(group), j]), AXES, found[j], n) for j in range(1, size)]
        own = take(x, w[tuple(group), 0]).astype(f32)
        x = sum((g.astype(f32) for g in got), own).astype(bf16)
        done.append(group)
    for group in reversed(done):
        x = join(x, group, w, n)
    found = members([m * nt for m in near_masks(nb)])
    own = [x] + [swap(x, AXES, m, n) for m in found[:0:-1]][::-1]
    return own, [swap(x, AXES, nt, n) for x in own]


def hot(ids, width, dtype):
    return (ids[:, None] == jnp.arange(width, dtype=jnp.int32)[None, :]).astype(dtype)


def nt_dot(a, b):
    return lax.dot_general(a, b, (((1,), (1,)), ((), ())), preferred_element_type=f32)


def tn_dot(a, b, preferred_element_type=f32):
    return lax.dot_general(
        a, b, (((0,), (0,)), ((), ())), preferred_element_type=preferred_element_type
    )


def hot_columns(ids, width):
    found = lax.broadcasted_iota(jnp.int32, (width, ids.shape[1]), 0) == ids
    return jnp.where(found, 1.0, 0.0).astype(bf16)


def gelu_pair(x):
    c = 0.7978845608028654
    square = x * x
    t = jnp.tanh(c * (x + 0.044715 * (square * x)))
    half = 0.5 * (1.0 + t)
    slope = half + (0.5 * x) * ((1.0 - t) * (1.0 + t)) * (c + (3.0 * 0.044715 * c) * square)
    return (x * half).astype(bf16), slope


def forward(rows, one_hot, w_in, bias, w_out, dot=tn_dot):
    embed = w_out.shape[1]
    table = bias[...]
    table = jnp.concatenate([table, jnp.zeros((embed - table.shape[0], table.shape[1]), f32)], 0)
    added = None
    for _ in range(3):
        piece = table.astype(bf16)
        table = table - piece.astype(f32)
        part = dot(one_hot, piece, preferred_element_type=f32)
        added = part if added is None else added + part
    pre = jnp.dot(rows, w_in[...], preferred_element_type=f32) + added
    hidden, slope = gelu_pair(pre)
    latent = jnp.dot(hidden, w_out[...], preferred_element_type=f32)
    radius = jnp.sqrt(jnp.sum(latent * latent, axis=1, keepdims=True) + epsilon)
    return (latent / radius).astype(bf16), latent, hidden, slope, pre


def front_kernel(count, *refs):
    held, (unit_ref, wide_ref), scratch, sems = (
        refs[:count],
        refs[count : count + 2],
        refs[count + 2 : -1],
        refs[-1],
    )
    copies = [
        pltpu.make_async_copy(src, dst, sems.at[i]) for i, (src, dst) in enumerate(zip(held, scratch))
    ]
    for copy in copies:
        copy.start()
    w_in, bias, w_out, ids, rows = scratch
    for copy in copies:
        copy.wait()
    embed, channels = w_out.shape[1], w_in.shape[0]
    one_hot = hot_columns(ids[...], embed)
    unit_ref[...] = forward(rows[...], one_hot, w_in, bias, w_out)[0]
    wide_ref[:, :channels] = rows[...]
    wide_ref[:, channels:] = one_hot.astype(f32).T.astype(bf16)


def refs_kernel(rows, ids, w_in, bias, w_out, unit, latent, hidden, slope):
    values = forward(rows[...], hot_columns(ids[...], w_out.shape[1]), w_in, bias, w_out)
    for out, value in zip((unit, latent, hidden, slope), values):
        out[...] = value


def near_forward_kernel(wide, w_in, bias, w_out, latent, hidden, slope):
    channels = w_in.shape[0]
    values = forward(wide[:, :channels], wide[:, channels:], w_in, bias, w_out, jnp.dot)
    for out, value in zip((latent, hidden, slope), values[1:]):
        out[...] = value


def exponent_kernel(u_ref, pool_ref, exponent_ref):
    scores = nt_dot(u_ref[...], pool_ref[...]) / logit_sharpness_divisor
    exponent_ref[...] = jnp.exp(scores - shift_bound)


def positives_kernel(here_ref, owner, own, ids, w_in, bias, w_out, *refs):
    gots, (rows_ref, unit_ref, latent_ref, pre_ref) = refs[:-4], refs[-4:]
    held = jnp.where(owner[...] == here_ref[0], 1.0, 0.0)
    held = jnp.broadcast_to(held, (w_out.shape[1], held.shape[1])).T[:, :1] > 0.5
    rows = gots[0][...]
    for got in gots[1:]:
        rows = rows + got[...]
    rows = jnp.where(held, own[...].astype(f32), rows.astype(f32)).astype(bf16)
    rows_ref[...] = rows
    values = forward(rows, hot_columns(ids[...], w_out.shape[1]), w_in, bias, w_out)
    unit_ref[...], latent_ref[...], pre_ref[...] = values[0], values[1], values[4]


def score_kernel(scale, order, me_ref, u_ref, v_ref, pool_ref, exponent_ref, *refs):
    kept_ref, sent_ref, loss_ref, grad_ref, grad_pos, share_ref = refs
    v = v_ref[...]
    u, pool = u_ref[...], pool_ref[...]
    uf, vf = u.astype(f32), v.astype(f32)
    pos_score = jnp.sum(uf * vf, axis=1, keepdims=True) / logit_sharpness_divisor
    exponent = exponent_ref[...]
    pos_exp = jnp.exp(pos_score - shift_bound)
    normalizer = pos_exp + jnp.sum(exponent, axis=1, keepdims=True)
    weights = (exponent / normalizer).astype(bf16)
    share_ref[...] = scale * tn_dot(weights, u)
    rows = kept_ref.shape[0] // len(order)
    for i, k in enumerate(order):
        at = pl.multiple_of((me_ref[0] ^ k) * rows, rows)
        kept_ref[i * rows : (i + 1) * rows, :] = share_ref[pl.ds(at, rows), :]
        at = pl.multiple_of((me_ref[0] ^ k ^ 1) * rows, rows)
        sent_ref[i * rows : (i + 1) * rows, :] = share_ref[pl.ds(at, rows), :].astype(bf16)
    loss = jnp.log(normalizer) + shift_bound - pos_score
    loss_ref[...] = jnp.broadcast_to(loss, uf.shape).T[:1]
    pull = pos_exp / normalizer - 1.0
    grad_ref[...] = scale * (jnp.dot(weights, pool, preferred_element_type=f32) + pull * vf)
    grad_pos[...] = scale * pull * uf


def pulled_back(latent, slope, grad_unit, w_out):
    power = jnp.sum(latent * latent, axis=1, keepdims=True) + epsilon
    radius = jnp.sqrt(power)
    inner = jnp.sum(latent * grad_unit, axis=1, keepdims=True)
    grad_latent = ((grad_unit - latent * (inner / (radius * radius))) / radius).astype(bf16)
    return grad_latent, (nt_dot(grad_latent, w_out[...]) * slope).astype(bf16)


def piece_sizes(channels, embed, animals, pieces):
    return channels // (2 * pieces), embed // (2 * pieces), -(-animals // 8) * 8


def two_sets_kernel(
    pieces, animals, ids, a_rows, a_latent, a_hidden, a_slope, a_grad, b_rows, b_latent, b_pre, b_grad, w_out, total
):
    embed, channels = w_out.shape[1], a_rows.shape[1]
    one_hot = hot_columns(ids[...], embed)
    a_latent_grad, a_pre_grad = pulled_back(a_latent[...], a_slope[...], a_grad[...], w_out)
    b_hidden, b_slope = gelu_pair(b_pre[...])
    b_latent_grad, b_pre_grad = pulled_back(b_latent[...], b_slope, b_grad[...], w_out)
    big = tn_dot(a_rows[...], a_pre_grad) + tn_dot(b_rows[...], b_pre_grad)
    low = tn_dot(a_latent_grad, a_hidden[...]) + tn_dot(b_latent_grad, b_hidden)
    animal = jnp.dot(one_hot, a_pre_grad, preferred_element_type=f32)
    animal = animal + jnp.dot(one_hot, b_pre_grad, preferred_element_type=f32)
    top, small, biases = piece_sizes(channels, embed, animals, pieces)
    for i in range(2 * pieces):
        at = i * (top + small + biases)
        total[at : at + top, :] = big[i * top : (i + 1) * top]
        total[at + top : at + top + small, :] = low[i * small : (i + 1) * small]
        total[at + top + small : at + top + small + biases, :] = animal[:biases]


def negatives_kernel(pieces, animals, wide, latent, hidden, slope, grad, w_out, before, total):
    embed = w_out.shape[1]
    channels = wide.shape[1] - embed
    grad_latent, grad_pre = pulled_back(latent[...], slope[...], grad[...], w_out)
    big = tn_dot(wide[:, :channels], grad_pre)
    low = tn_dot(grad_latent, hidden[...])
    animal = tn_dot(wide[:, channels:], grad_pre)
    top, small, biases = piece_sizes(channels, embed, animals, pieces)
    for i in range(2 * pieces):
        at = i * (top + small + biases)
        ends = (at, at + top, at + top + small, at + top + small + biases)
        terms = (big[i * top : (i + 1) * top], low[i * small : (i + 1) * small], animal[:biases])
        for start, end, term in zip(ends, ends[1:], terms):
            total[start:end, :] = (before[start:end, :] + term).astype(bf16)


def piece_kernel(*refs):
    terms, out = refs[:-1], refs[-1]
    got = terms[0][...].astype(f32)
    for term in terms[1:]:
        got = got + term[...].astype(f32)
    blocks, _, width = out.shape
    for i in range(blocks):
        out[i] = got[:, i * width : (i + 1) * width].astype(bf16)


def finish_kernel(pieces, core_ref, *refs):
    places, own, other = (refs[i * pieces : (i + 1) * pieces] for i in range(3))
    grad_w_in, grad_w_out, grad_bias, lows, bias_rows = refs[3 * pieces :]
    animals = grad_bias.shape[0]
    top, small, biases = piece_sizes(grad_w_in.shape[0], grad_w_out.shape[1], animals, pieces)
    blocks, _, width = own[0].shape
    for half, held in ((core_ref[0], own), (1 - core_ref[0], other)):
        for place_ref, piece in zip(places, held):
            at = half * pieces + place_ref[0]
            tops = pl.ds(pl.multiple_of(at * top, top), top)
            rows = pl.ds(pl.multiple_of(at * small, small), small)
            last = pl.ds(pl.multiple_of(at * biases, biases), biases)
            for i in range(blocks):
                columns = slice(i * width, (i + 1) * width)
                grad_w_in[tops, columns] = piece[i, :top, :]
                lows[rows, columns] = piece[i, top : top + small, :].astype(f32)
                bias_rows[last, columns] = piece[i, top + small :, :].astype(f32)
    grad_w_out[...] = lows[...].T
    grad_bias[...] = bias_rows[:animals, :]


def call(kernel, name, out, *args, scalars=0, limit=12, space=pltpu.VMEM, scratch=()):
    whole = pl.BlockSpec(memory_space=pltpu.VMEM)
    given = pl.BlockSpec(memory_space=space)
    shapes = [jax.ShapeDtypeStruct(*o) for o in out]
    return pl.pallas_call(
        kernel,
        name=name,
        out_shape=shapes,
        in_specs=[pl.BlockSpec(memory_space=pltpu.SMEM)] * scalars + [given] * (len(args) - scalars),
        out_specs=[whole] * len(out),
        scratch_shapes=list(scratch),
        compiler_params=pltpu.CompilerParams(vmem_limit_bytes=limit * 2**20),
    )(*args)


def sets(rows, embed, width):
    return [((rows, embed), f32), ((rows, width), bf16), ((rows, width), f32)]


def slots(owner, row, nt, me_t):
    refs = row.shape[0]
    cap = 2 * refs // nt
    owner_hot = hot(owner, nt, jnp.int32)
    slot = jnp.sum((jnp.cumsum(owner_hot, axis=0) - owner_hot) * owner_hot, axis=1)
    found = []
    for k in range(1, nt):
        wanted = owner == (me_t ^ k)
        pick = wanted[None, :] & (slot[None, :] == jnp.arange(cap, dtype=jnp.int32)[:, None])
        found.append((pick, jnp.max(jnp.where(pick, row[None, :], -1), axis=1)[None, :]))
    return found


def pick_kernel(row, recording, rows):
    one_hot = hot_columns(row[...], recording.shape[0])
    rows[...] = tn_dot(one_hot, recording[...]).astype(bf16)


def pick_rows(row, recording):
    out = [((row.shape[1], recording.shape[1]), bf16)]
    return call(pick_kernel, "pick", out, row, recording)[0]


def on_device(
    ref_rows,
    neg_rows,
    recording,
    pos_owner,
    pos_row,
    ref_animal,
    neg_animal,
    w_in,
    bias_animal,
    w_out,
):
    refs = ref_rows.shape[0]
    channels = w_in.shape[0]
    embed = w_out.shape[1]
    animals = bias_animal.shape[0]
    nt = lax.axis_size("tm")
    nb = lax.axis_size("batch")
    n = nt * nb
    me_b = lax.axis_index("batch")
    me_t = lax.axis_index("tm")
    w = positions(nb, nt, me_b, me_t)
    here, *found = lax.optimization_barrier((me_t.reshape(1), *w.values()))
    w = dict(zip(w, found))

    owner, row = pos_owner.reshape(1, refs), pos_row.reshape(1, refs)
    ref_ids, neg_ids = ref_animal[None, :], neg_animal[None, :]
    if nt == 2:
        asks = [(None, row)]
    else:
        asks = slots(pos_owner[:, 0], pos_row, nt, me_t)
    asked = [swap(ask, "tm", k, nt) for k, (_, ask) in enumerate(asks, 1)]
    weights = (w_in, bias_animal, w_out)
    hidden_width = w_in.shape[1]
    inputs = (*weights, neg_ids, neg_rows)
    inputs = [pltpu.with_memory_space_constraint(x, pltpu.HBM) for x in inputs]
    negs = neg_rows.shape[0]
    here, *inputs = lax.optimization_barrier((here, *inputs))
    neg_unit, wide = call(
        functools.partial(front_kernel, len(inputs)),
        "front",
        [((negs, embed), bf16), ((negs, channels + embed), bf16)],
        *inputs,
        space=pltpu.HBM,
        scratch=[pltpu.VMEM(x.shape, x.dtype) for x in inputs]
        + [pltpu.SemaphoreType.DMA((len(inputs),))],
    )
    found = [pick_rows(ask, recording) for ask in asked]
    neg_unit, found, wide = lax.optimization_barrier((neg_unit, found, wide))
    got = [swap(f, "tm", k, nt) for k, f in enumerate(found, 1)]
    near = near_masks(nb)
    shared = wide_masks(nb)
    wide = spread(wide, shared[:1], nb)
    pool, wide, (ref_rows, row) = gather_batch(neg_unit, nb, w, wide, (ref_rows, row))
    wide = spread(wide, shared[1:], nb)
    u, ref_latent, ref_hidden, ref_slope = call(
        refs_kernel,
        "refs",
        [((refs, embed), bf16), *sets(refs, embed, hidden_width)],
        *(ref_rows, ref_ids, *weights),
    )
    own = pick_rows(row, recording)
    got = [
        g if pick is None else jnp.dot(pick.T.astype(bf16), g, preferred_element_type=bf16)
        for (pick, _), g in zip(asks, got)
    ]

    scale = float(refs * n) ** (-0.5) / logit_sharpness_divisor
    exponent = call(
        exponent_kernel,
        "exponents",
        [((refs, pool.shape[0]), f32)],
        *(u, pool),
        limit=max(12, 12 * refs * pool.shape[0] >> 20),
    )[0]
    pos_rows, v, pos_latent, pos_pre = call(
        positives_kernel,
        "positives",
        [(ref_rows.shape, bf16), (u.shape, bf16), (u.shape, f32), ((refs, hidden_width), f32)],
        *(here, owner, own, ref_ids, *weights, *got),
        scalars=1,
    )
    half = pool.shape[0] // 2
    out = [((half, embed), f32), ((half, embed), bf16), ((1, refs), f32)]
    out += [(u.shape, f32), (u.shape, f32)]
    kept, sent, loss, grad_ref, grad_pos = call(
        functools.partial(score_kernel, scale, kept_order(nb)),
        "scores",
        out,
        *(w["b", 0].reshape(1), u, v, pool, exponent),
        scalars=1,
        limit=max(12, 20 * refs * pool.shape[0] >> 20),
        scratch=[pltpu.VMEM((pool.shape[0], embed), f32)],
    )
    pieces = 1 << len(near)
    piece_rows = sum(piece_sizes(channels, embed, animals, pieces))
    total = call(
        functools.partial(two_sets_kernel, pieces, animals),
        "backward",
        [((2 * pieces * piece_rows, hidden_width), f32)],
        ref_ids,
        *(ref_rows, ref_latent, ref_hidden, ref_slope, grad_ref),
        *(pos_rows, pos_latent, pos_pre, grad_pos),
        w_out,
    )[0]
    near_values = call(
        near_forward_kernel,
        "near_forward",
        sets(wide.shape[0], embed, hidden_width),
        *(wide, *weights),
    )
    mine = scatter_batch(kept, sent, nb)
    total = call(
        functools.partial(negatives_kernel, pieces, animals),
        "negatives",
        [(total.shape, bf16)],
        *(wide, *near_values, mine, w_out, total),
    )[0]
    parts = split_pair(total, nb, nt, w)
    total = call(
        piece_kernel,
        "piece",
        [((hidden_width // 128, piece_rows, 128), bf16)],
        *split_near(parts, nb, nt),
    )[0]
    own, other = finish_sum(total, nb, nt, w)
    places = [w[tuple(m * nt for m in near), j].reshape(1) for j in range(pieces)]
    grad_w_in, grad_w_out, grad_bias = call(
        functools.partial(finish_kernel, pieces),
        "finish",
        [(w_in.shape, bf16), (w_out.shape, f32), (bias_animal.shape, f32)],
        w[(nt,), 0].reshape(1),
        *(*places, *own, *other),
        scalars=1 + pieces,
        scratch=[
            pltpu.VMEM((embed, hidden_width), f32),
            pltpu.VMEM((2 * pieces * piece_sizes(channels, embed, animals, pieces)[2], hidden_width), f32),
        ],
    )
    return (loss.reshape(refs), grad_w_in, grad_w_out, grad_bias)


def solution(mesh):
    in_specs = (
        P(("batch", "tm"), None),
        P(("batch", "tm"), None),
        P("tm", None),
        P(("batch", "tm"), None),
        P(("batch", "tm")),
        P(("batch", "tm")),
        P(("batch", "tm")),
        P(),
        P(),
        P(),
    )
    out_specs = (P(("batch", "tm")), P(), P(), P())
    return jax.shard_map(
        on_device, mesh=mesh, in_specs=in_specs, out_specs=out_specs, check_vma=False
    )
```

```python
import functools

import jax
import jax.numpy as jnp
from jax import lax
from jax.experimental import pallas as pl
from jax.experimental.pallas import tpu as pltpu
from jax.sharding import PartitionSpec as P

logit_sharpness_divisor = 0.1
shift_bound = 10.0
epsilon = 1e-06
AXES = ("batch", "tm")
bf16 = jnp.bfloat16
f32 = jnp.float32


def swap(x, axes, mask, n):
    return lax.ppermute(x, axes, [(i, i ^ mask) for i in range(n)])


def batch_masks(nb):
    return [1 << i for i in range(nb.bit_length() - 1)]


def gather_batch(x, nb, w, wide, later):
    masks = batch_masks(nb)
    order = masks[-1:] + masks[1:-2][::-1] + masks[-2:-1] + masks[:1]
    rows = x.shape[0]
    parts = {0: x}
    for m in order:
        keys = list(parts)
        block = jnp.concatenate([parts[k] for k in keys], 0) if len(keys) > 1 else parts[keys[0]]
        if len(keys) == 2:
            block, later = lax.optimization_barrier((block, later))
        if m == masks[-2]:
            block, wide = lax.optimization_barrier((block, wide))
        got = swap(block, "batch", m, nb)
        for i, k in enumerate(keys):
            parts[k ^ m] = got[i * rows : (i + 1) * rows]
    out = jnp.zeros((nb,) + x.shape, x.dtype)
    for k, part in parts.items():
        out = put(out, part, w["b", k])
    return out.reshape((nb * rows,) + x.shape[1:]), wide, later


def near_masks(nb):
    return batch_masks(nb)[1:3]


def spread(x, masks, nb):
    for m in masks:
        x = jnp.concatenate([x, swap(x, "batch", m, nb)], 0)
    return x


def wide_masks(nb):
    return batch_masks(nb)[-2:]


def kept_order(nb):
    masks = batch_masks(nb)[1:-2]
    high = [sum(m for i, m in enumerate(masks) if j >> i & 1) for j in range(1 << len(masks))]
    return [h ^ k for h in high for k in members(wide_masks(nb))]


def scatter_batch(kept, sent, nb):
    masks = batch_masks(nb)
    x = kept + swap(sent, "batch", masks[0], nb).astype(f32)
    for m in masks[1:-2][::-1]:
        half = x.shape[0] // 2
        x = x[:half] + swap(x[half:].astype(bf16), "batch", m, nb).astype(f32)
    return x


def far_groups(nb, nt):
    rest = [m * nt for m in batch_masks(nb)[3:]] + [1 << i for i in range(nt.bit_length() - 1)]
    return [rest[i : i + 2] for i in range(0, len(rest), 2)]


def members(group):
    found = [0]
    for m in group:
        found = found + [a ^ m for a in found]
    return found


def place(me, group):
    return sum(jnp.where((me & m) != 0, 1 << i, 0) for i, m in enumerate(group))


def take(x, i):
    return lax.dynamic_index_in_dim(x, i, 0, False, allow_negative_indices=False)


def put(x, part, i):
    return lax.dynamic_update_index_in_dim(x, part, i, 0, allow_negative_indices=False)


def positions(nb, nt, me_b, me_t):
    me = me_b * nt + me_t
    near = [m * nt for m in near_masks(nb)]
    w = {("b", k): me_b ^ k for k in range(nb)}
    for group in [[nt], near] + far_groups(nb, nt):
        p = place(me, group)
        for j in range(1 << len(group)):
            w[tuple(group), j] = p ^ j
    return w


def split_pair(x, nb, nt, w):
    near = [m * nt for m in near_masks(nb)]
    n, found = nb * nt, members(near)
    halves = x.reshape(2, x.shape[0] // 2, x.shape[1])
    got = swap(take(halves, w[(nt,), 1]), AXES, nt, n)
    own = take(halves, w[(nt,), 0])
    x = (own.astype(f32) + got.astype(f32)).astype(bf16)
    xs = x.reshape(len(found), x.shape[0] // len(found), x.shape[1])
    return [take(xs, w[tuple(near), j]) for j in range(len(found))]


def split_near(pieces, nb, nt):
    found = members([m * nt for m in near_masks(nb)])
    return pieces[:1] + [swap(x, AXES, m, nb * nt) for x, m in zip(pieces[1:], found[1:])]


def join(x, group, w, n):
    found = members(group)
    out = jnp.zeros((len(found),) + x.shape, x.dtype)
    got = [x] + [swap(x, AXES, m, n) for m in found[1:]]
    for j, g in enumerate(got):
        out = put(out, g, w[tuple(group), j])
    return out


def finish_sum(x, nb, nt, w):
    n = nb * nt
    done = []
    for group in far_groups(nb, nt):
        found = members(group)
        size = len(found)
        if x.ndim == 2 or x.shape[0] != size:
            terms = [x.astype(f32)] + [swap(x, AXES, m, n).astype(f32) for m in found[1:]]
            while len(terms) > 1:
                terms = [a + b for a, b in zip(terms[::2], terms[1::2])]
            x = terms[0].astype(bf16)
            continue
        got = [swap(take(x, w[tuple(group), j]), AXES, found[j], n) for j in range(1, size)]
        own = take(x, w[tuple(group), 0]).astype(f32)
        x = sum((g.astype(f32) for g in got), own).astype(bf16)
        done.append(group)
    for group in reversed(done):
        x = join(x, group, w, n)
    found = members([m * nt for m in near_masks(nb)])
    own = [x] + [swap(x, AXES, m, n) for m in found[:0:-1]][::-1]
    return own, [swap(x, AXES, nt, n) for x in own]


def hot(ids, width, dtype):
    return (ids[:, None] == jnp.arange(width, dtype=jnp.int32)[None, :]).astype(dtype)


def nt_dot(a, b):
    return lax.dot_general(a, b, (((1,), (1,)), ((), ())), preferred_element_type=f32)


def tn_dot(a, b, preferred_element_type=f32):
    return lax.dot_general(
        a, b, (((0,), (0,)), ((), ())), preferred_element_type=preferred_element_type
    )


def hot_columns(ids, width):
    found = lax.broadcasted_iota(jnp.int32, (width, ids.shape[1]), 0) == ids
    return jnp.where(found, 1.0, 0.0).astype(bf16)


def gelu_pair(x):
    c = 0.7978845608028654
    square = x * x
    t = jnp.tanh(c * (x + 0.044715 * (square * x)))
    half = 0.5 * (1.0 + t)
    slope = half + (0.5 * x) * ((1.0 - t) * (1.0 + t)) * (c + (3.0 * 0.044715 * c) * square)
    return (x * half).astype(bf16), slope


def forward(rows, one_hot, w_in, bias, w_out, dot=tn_dot):
    embed = w_out.shape[1]
    table = bias[...]
    table = jnp.concatenate([table, jnp.zeros((embed - table.shape[0], table.shape[1]), f32)], 0)
    added = None
    for _ in range(3):
        piece = table.astype(bf16)
        table = table - piece.astype(f32)
        part = dot(one_hot, piece, preferred_element_type=f32)
        added = part if added is None else added + part
    pre = jnp.dot(rows, w_in[...], preferred_element_type=f32) + added
    hidden, slope = gelu_pair(pre)
    latent = jnp.dot(hidden, w_out[...], preferred_element_type=f32)
    radius = jnp.sqrt(jnp.sum(latent * latent, axis=1, keepdims=True) + epsilon)
    return (latent / radius).astype(bf16), latent, hidden, slope, pre


def front_kernel(count, *refs):
    held, (unit_ref, wide_ref), scratch, sems = (
        refs[:count],
        refs[count : count + 2],
        refs[count + 2 : -1],
        refs[-1],
    )
    copies = [
        pltpu.make_async_copy(src, dst, sems.at[i]) for i, (src, dst) in enumerate(zip(held, scratch))
    ]
    for copy in copies:
        copy.start()
    w_in, bias, w_out, ids, rows = scratch
    for copy in copies:
        copy.wait()
    embed, channels = w_out.shape[1], w_in.shape[0]
    one_hot = hot_columns(ids[...], embed)
    unit_ref[...] = forward(rows[...], one_hot, w_in, bias, w_out)[0]
    wide_ref[:, :channels] = rows[...]
    wide_ref[:, channels:] = one_hot.astype(f32).T.astype(bf16)


def refs_kernel(rows, ids, w_in, bias, w_out, unit, latent, hidden, slope):
    values = forward(rows[...], hot_columns(ids[...], w_out.shape[1]), w_in, bias, w_out)
    for out, value in zip((unit, latent, hidden, slope), values):
        out[...] = value


def near_forward_kernel(wide, w_in, bias, w_out, latent, hidden, slope):
    channels = w_in.shape[0]
    values = forward(wide[:, :channels], wide[:, channels:], w_in, bias, w_out, jnp.dot)
    for out, value in zip((latent, hidden, slope), values[1:]):
        out[...] = value


def exponent_kernel(u_ref, pool_ref, exponent_ref):
    scores = nt_dot(u_ref[...], pool_ref[...]) / logit_sharpness_divisor
    exponent_ref[...] = jnp.exp(scores - shift_bound)


def positives_kernel(here_ref, owner, own, ids, w_in, bias, w_out, *refs):
    gots, (rows_ref, unit_ref, latent_ref, pre_ref) = refs[:-4], refs[-4:]
    held = jnp.where(owner[...] == here_ref[0], 1.0, 0.0)
    held = jnp.broadcast_to(held, (w_out.shape[1], held.shape[1])).T[:, :1] > 0.5
    rows = gots[0][...]
    for got in gots[1:]:
        rows = rows + got[...]
    rows = jnp.where(held, own[...].astype(f32), rows.astype(f32)).astype(bf16)
    rows_ref[...] = rows
    values = forward(rows, hot_columns(ids[...], w_out.shape[1]), w_in, bias, w_out)
    unit_ref[...], latent_ref[...], pre_ref[...] = values[0], values[1], values[4]


def score_kernel(scale, order, me_ref, u_ref, v_ref, pool_ref, exponent_ref, *refs):
    kept_ref, sent_ref, loss_ref, grad_ref, grad_pos, share_ref = refs
    v = v_ref[...]
    u, pool = u_ref[...], pool_ref[...]
    uf, vf = u.astype(f32), v.astype(f32)
    pos_score = jnp.sum(uf * vf, axis=1, keepdims=True) / logit_sharpness_divisor
    exponent = exponent_ref[...]
    pos_exp = jnp.exp(pos_score - shift_bound)
    normalizer = pos_exp + jnp.sum(exponent, axis=1, keepdims=True)
    weights = (exponent / normalizer).astype(bf16)
    share_ref[...] = scale * tn_dot(weights, u)
    rows = kept_ref.shape[0] // len(order)
    for i, k in enumerate(order):
        at = pl.multiple_of((me_ref[0] ^ k) * rows, rows)
        kept_ref[i * rows : (i + 1) * rows, :] = share_ref[pl.ds(at, rows), :]
        at = pl.multiple_of((me_ref[0] ^ k ^ 1) * rows, rows)
        sent_ref[i * rows : (i + 1) * rows, :] = share_ref[pl.ds(at, rows), :].astype(bf16)
    loss = jnp.log(normalizer) + shift_bound - pos_score
    loss_ref[...] = jnp.broadcast_to(loss, uf.shape).T[:1]
    pull = pos_exp / normalizer - 1.0
    grad_ref[...] = scale * (jnp.dot(weights, pool, preferred_element_type=f32) + pull * vf)
    grad_pos[...] = scale * pull * uf


def pulled_back(latent, slope, grad_unit, w_out):
    power = jnp.sum(latent * latent, axis=1, keepdims=True) + epsilon
    radius = jnp.sqrt(power)
    inner = jnp.sum(latent * grad_unit, axis=1, keepdims=True)
    grad_latent = ((grad_unit - latent * (inner / (radius * radius))) / radius).astype(bf16)
    return grad_latent, (nt_dot(grad_latent, w_out[...]) * slope).astype(bf16)


def piece_sizes(channels, embed, animals, pieces):
    return channels // (2 * pieces), embed // (2 * pieces), -(-animals // 8) * 8


def two_sets_kernel(
    pieces, animals, ids, a_rows, a_latent, a_hidden, a_slope, a_grad, b_rows, b_latent, b_pre, b_grad, w_out, total
):
    embed, channels = w_out.shape[1], a_rows.shape[1]
    one_hot = hot_columns(ids[...], embed)
    a_latent_grad, a_pre_grad = pulled_back(a_latent[...], a_slope[...], a_grad[...], w_out)
    b_hidden, b_slope = gelu_pair(b_pre[...])
    b_latent_grad, b_pre_grad = pulled_back(b_latent[...], b_slope, b_grad[...], w_out)
    big = tn_dot(a_rows[...], a_pre_grad) + tn_dot(b_rows[...], b_pre_grad)
    low = tn_dot(a_latent_grad, a_hidden[...]) + tn_dot(b_latent_grad, b_hidden)
    animal = jnp.dot(one_hot, a_pre_grad, preferred_element_type=f32)
    animal = animal + jnp.dot(one_hot, b_pre_grad, preferred_element_type=f32)
    top, small, biases = piece_sizes(channels, embed, animals, pieces)
    for i in range(2 * pieces):
        at = i * (top + small + biases)
        total[at : at + top, :] = big[i * top : (i + 1) * top]
        total[at + top : at + top + small, :] = low[i * small : (i + 1) * small]
        total[at + top + small : at + top + small + biases, :] = animal[:biases]


def negatives_kernel(pieces, animals, wide, latent, hidden, slope, grad, w_out, before, total):
    embed = w_out.shape[1]
    channels = wide.shape[1] - embed
    grad_latent, grad_pre = pulled_back(latent[...], slope[...], grad[...], w_out)
    big = tn_dot(wide[:, :channels], grad_pre)
    low = tn_dot(grad_latent, hidden[...])
    animal = tn_dot(wide[:, channels:], grad_pre)
    top, small, biases = piece_sizes(channels, embed, animals, pieces)
    for i in range(2 * pieces):
        at = i * (top + small + biases)
        ends = (at, at + top, at + top + small, at + top + small + biases)
        terms = (big[i * top : (i + 1) * top], low[i * small : (i + 1) * small], animal[:biases])
        for start, end, term in zip(ends, ends[1:], terms):
            total[start:end, :] = (before[start:end, :] + term).astype(bf16)


def piece_kernel(*refs):
    terms, out = refs[:-1], refs[-1]
    got = terms[0][...].astype(f32)
    for term in terms[1:]:
        got = got + term[...].astype(f32)
    blocks, _, width = out.shape
    for i in range(blocks):
        out[i] = got[:, i * width : (i + 1) * width].astype(bf16)


def finish_kernel(pieces, core_ref, *refs):
    places, own, other = (refs[i * pieces : (i + 1) * pieces] for i in range(3))
    grad_w_in, grad_w_out, grad_bias, lows, bias_rows = refs[3 * pieces :]
    animals = grad_bias.shape[0]
    top, small, biases = piece_sizes(grad_w_in.shape[0], grad_w_out.shape[1], animals, pieces)
    blocks, _, width = own[0].shape
    for half, held in ((core_ref[0], own), (1 - core_ref[0], other)):
        for place_ref, piece in zip(places, held):
            at = half * pieces + place_ref[0]
            tops = pl.ds(pl.multiple_of(at * top, top), top)
            rows = pl.ds(pl.multiple_of(at * small, small), small)
            last = pl.ds(pl.multiple_of(at * biases, biases), biases)
            for i in range(blocks):
                columns = slice(i * width, (i + 1) * width)
                grad_w_in[tops, columns] = piece[i, :top, :]
                lows[rows, columns] = piece[i, top : top + small, :].astype(f32)
                bias_rows[last, columns] = piece[i, top + small :, :].astype(f32)
    grad_w_out[...] = lows[...].T
    grad_bias[...] = bias_rows[:animals, :]


def call(kernel, name, out, *args, scalars=0, limit=12, space=pltpu.VMEM, scratch=()):
    whole = pl.BlockSpec(memory_space=pltpu.VMEM)
    given = pl.BlockSpec(memory_space=space)
    shapes = [jax.ShapeDtypeStruct(*o) for o in out]
    return pl.pallas_call(
        kernel,
        name=name,
        out_shape=shapes,
        in_specs=[pl.BlockSpec(memory_space=pltpu.SMEM)] * scalars + [given] * (len(args) - scalars),
        out_specs=[whole] * len(out),
        scratch_shapes=list(scratch),
        compiler_params=pltpu.CompilerParams(vmem_limit_bytes=limit * 2**20),
    )(*args)


def sets(rows, embed, width):
    return [((rows, embed), f32), ((rows, width), bf16), ((rows, width), f32)]


def slots(owner, row, nt, me_t):
    refs = row.shape[0]
    cap = 2 * refs // nt
    owner_hot = hot(owner, nt, jnp.int32)
    slot = jnp.sum((jnp.cumsum(owner_hot, axis=0) - owner_hot) * owner_hot, axis=1)
    found = []
    for k in range(1, nt):
        wanted = owner == (me_t ^ k)
        pick = wanted[None, :] & (slot[None, :] == jnp.arange(cap, dtype=jnp.int32)[:, None])
        found.append((pick, jnp.max(jnp.where(pick, row[None, :], -1), axis=1)[None, :]))
    return found


def pick_kernel(row, recording, rows):
    one_hot = hot_columns(row[...], recording.shape[0])
    rows[...] = tn_dot(one_hot, recording[...]).astype(bf16)


def pick_rows(row, recording):
    out = [((row.shape[1], recording.shape[1]), bf16)]
    return call(pick_kernel, "pick", out, row, recording)[0]


def on_device(
    ref_rows,
    neg_rows,
    recording,
    pos_owner,
    pos_row,
    ref_animal,
    neg_animal,
    w_in,
    bias_animal,
    w_out,
):
    refs = ref_rows.shape[0]
    channels = w_in.shape[0]
    embed = w_out.shape[1]
    animals = bias_animal.shape[0]
    nt = lax.axis_size("tm")
    nb = lax.axis_size("batch")
    n = nt * nb
    me_b = lax.axis_index("batch")
    me_t = lax.axis_index("tm")
    w = positions(nb, nt, me_b, me_t)
    here, *found = lax.optimization_barrier((me_t.reshape(1), *w.values()))
    w = dict(zip(w, found))

    owner, row = pos_owner.reshape(1, refs), pos_row.reshape(1, refs)
    ref_ids, neg_ids = ref_animal[None, :], neg_animal[None, :]
    if nt == 2:
        asks = [(None, row)]
    else:
        asks = slots(pos_owner[:, 0], pos_row, nt, me_t)
    asked = [swap(ask, "tm", k, nt) for k, (_, ask) in enumerate(asks, 1)]
    weights = (w_in, bias_animal, w_out)
    hidden_width = w_in.shape[1]
    inputs = (*weights, neg_ids, neg_rows)
    inputs = [pltpu.with_memory_space_constraint(x, pltpu.HBM) for x in inputs]
    negs = neg_rows.shape[0]
    here, *inputs = lax.optimization_barrier((here, *inputs))
    neg_unit, wide = call(
        functools.partial(front_kernel, len(inputs)),
        "front",
        [((negs, embed), bf16), ((negs, channels + embed), bf16)],
        *inputs,
        space=pltpu.HBM,
        scratch=[pltpu.VMEM(x.shape, x.dtype) for x in inputs]
        + [pltpu.SemaphoreType.DMA((len(inputs),))],
    )
    found = [pick_rows(ask, recording) for ask in asked]
    neg_unit, found, wide = lax.optimization_barrier((neg_unit, found, wide))
    got = [swap(f, "tm", k, nt) for k, f in enumerate(found, 1)]
    near = near_masks(nb)
    shared = wide_masks(nb)
    wide = spread(wide, shared[:1], nb)
    pool, wide, (ref_rows, row) = gather_batch(neg_unit, nb, w, wide, (ref_rows, row))
    wide = spread(wide, shared[1:], nb)
    u, ref_latent, ref_hidden, ref_slope = call(
        refs_kernel,
        "refs",
        [((refs, embed), bf16), *sets(refs, embed, hidden_width)],
        *(ref_rows, ref_ids, *weights),
    )
    own = pick_rows(row, recording)
    got = [
        g if pick is None else jnp.dot(pick.T.astype(bf16), g, preferred_element_type=bf16)
        for (pick, _), g in zip(asks, got)
    ]

    scale = float(refs * n) ** (-0.5) / logit_sharpness_divisor
    exponent = call(
        exponent_kernel,
        "exponents",
        [((refs, pool.shape[0]), f32)],
        *(u, pool),
        limit=max(12, 12 * refs * pool.shape[0] >> 20),
    )[0]
    pos_rows, v, pos_latent, pos_pre = call(
        positives_kernel,
        "positives",
        [(ref_rows.shape, bf16), (u.shape, bf16), (u.shape, f32), ((refs, hidden_width), f32)],
        *(here, owner, own, ref_ids, *weights, *got),
        scalars=1,
    )
    half = pool.shape[0] // 2
    out = [((half, embed), f32), ((half, embed), bf16), ((1, refs), f32)]
    out += [(u.shape, f32), (u.shape, f32)]
    kept, sent, loss, grad_ref, grad_pos = call(
        functools.partial(score_kernel, scale, kept_order(nb)),
        "scores",
        out,
        *(w["b", 0].reshape(1), u, v, pool, exponent),
        scalars=1,
        limit=max(12, 20 * refs * pool.shape[0] >> 20),
        scratch=[pltpu.VMEM((pool.shape[0], embed), f32)],
    )
    pieces = 1 << len(near)
    piece_rows = sum(piece_sizes(channels, embed, animals, pieces))
    total = call(
        functools.partial(two_sets_kernel, pieces, animals),
        "backward",
        [((2 * pieces * piece_rows, hidden_width), f32)],
        ref_ids,
        *(ref_rows, ref_latent, ref_hidden, ref_slope, grad_ref),
        *(pos_rows, pos_latent, pos_pre, grad_pos),
        w_out,
    )[0]
    near_values = call(
        near_forward_kernel,
        "near_forward",
        sets(wide.shape[0], embed, hidden_width),
        *(wide, *weights),
    )
    mine = scatter_batch(kept, sent, nb)
    total = call(
        functools.partial(negatives_kernel, pieces, animals),
        "negatives",
        [(total.shape, bf16)],
        *(wide, *near_values, mine, w_out, total),
    )[0]
    parts = split_pair(total, nb, nt, w)
    total = call(
        piece_kernel,
        "piece",
        [((hidden_width // 128, piece_rows, 128), bf16)],
        *split_near(parts, nb, nt),
    )[0]
    own, other = finish_sum(total, nb, nt, w)
    places = [w[tuple(m * nt for m in near), j].reshape(1) for j in range(pieces)]
    grad_w_in, grad_w_out, grad_bias = call(
        functools.partial(finish_kernel, pieces),
        "finish",
        [(w_in.shape, bf16), (w_out.shape, f32), (bias_animal.shape, f32)],
        w[(nt,), 0].reshape(1),
        *(*places, *own, *other),
        scalars=1 + pieces,
        scratch=[
            pltpu.VMEM((embed, hidden_width), f32),
            pltpu.VMEM((2 * pieces * piece_sizes(channels, embed, animals, pieces)[2], hidden_width), f32),
        ],
    )
    return (loss.reshape(refs), grad_w_in, grad_w_out, grad_bias)


def solution(mesh):
    in_specs = (
        P(("batch", "tm"), None),
        P(("batch", "tm"), None),
        P("tm", None),
        P(("batch", "tm"), None),
        P(("batch", "tm")),
        P(("batch", "tm")),
        P(("batch", "tm")),
        P(),
        P(),
        P(),
    )
    out_specs = (P(("batch", "tm")), P(), P(), P())
    return jax.shard_map(
        on_device, mesh=mesh, in_specs=in_specs, out_specs=out_specs, check_vma=False
    )
```

```python
import functools

import jax
import jax.numpy as jnp
from jax import lax
from jax.experimental import pallas as pl
from jax.experimental.pallas import tpu as pltpu
from jax.sharding import PartitionSpec as P

logit_sharpness_divisor = 0.1
shift_bound = 10.0
epsilon = 1e-06
AXES = ("batch", "tm")
bf16 = jnp.bfloat16
f32 = jnp.float32


def swap(x, axes, mask, n):
    return lax.ppermute(x, axes, [(i, i ^ mask) for i in range(n)])


def batch_masks(nb):
    return [1 << i for i in range(nb.bit_length() - 1)]


def gather_batch(x, nb, w, wide, later):
    masks = batch_masks(nb)
    order = masks[-1:] + masks[1:-2][::-1] + masks[-2:-1] + masks[:1]
    rows = x.shape[0]
    parts = {0: x}
    for m in order:
        keys = list(parts)
        block = jnp.concatenate([parts[k] for k in keys], 0) if len(keys) > 1 else parts[keys[0]]
        if len(keys) == 2:
            block, later = lax.optimization_barrier((block, later))
        if m == masks[-2]:
            block, wide = lax.optimization_barrier((block, wide))
        got = swap(block, "batch", m, nb)
        for i, k in enumerate(keys):
            parts[k ^ m] = got[i * rows : (i + 1) * rows]
    out = jnp.zeros((nb,) + x.shape, x.dtype)
    for k, part in parts.items():
        out = put(out, part, w["b", k])
    return out.reshape((nb * rows,) + x.shape[1:]), wide, later


def near_masks(nb):
    return batch_masks(nb)[1:3]


def spread(x, masks, nb):
    for m in masks:
        x = jnp.concatenate([x, swap(x, "batch", m, nb)], 0)
    return x


def wide_masks(nb):
    return batch_masks(nb)[-2:]


def kept_order(nb):
    masks = batch_masks(nb)[1:-2]
    high = [sum(m for i, m in enumerate(masks) if j >> i & 1) for j in range(1 << len(masks))]
    return [h ^ k for h in high for k in members(wide_masks(nb))]


def scatter_batch(kept, sent, nb, wide):
    masks = batch_masks(nb)
    x = kept + swap(sent, "batch", masks[0], nb).astype(f32)
    for m in masks[1:-2][::-1]:
        half = x.shape[0] // 2
        send, wide = lax.optimization_barrier((x[half:].astype(bf16), wide))
        x = x[:half] + swap(send, "batch", m, nb).astype(f32)
    return x, wide


def far_groups(nb, nt):
    rest = [m * nt for m in batch_masks(nb)[3:]] + [1 << i for i in range(nt.bit_length() - 1)]
    return [rest[i : i + 2] for i in range(0, len(rest), 2)]


def members(group):
    found = [0]
    for m in group:
        found = found + [a ^ m for a in found]
    return found


def place(me, group):
    return sum(jnp.where((me & m) != 0, 1 << i, 0) for i, m in enumerate(group))


def take(x, i):
    return lax.dynamic_index_in_dim(x, i, 0, False, allow_negative_indices=False)


def put(x, part, i):
    return lax.dynamic_update_index_in_dim(x, part, i, 0, allow_negative_indices=False)


def positions(nb, nt, me_b, me_t):
    me = me_b * nt + me_t
    near = [m * nt for m in near_masks(nb)]
    w = {("b", k): me_b ^ k for k in range(nb)}
    for group in [[nt], near] + far_groups(nb, nt):
        p = place(me, group)
        for j in range(1 << len(group)):
            w[tuple(group), j] = p ^ j
    return w


def split_pair(x, nb, nt, w):
    near = [m * nt for m in near_masks(nb)]
    n, found = nb * nt, members(near)
    halves = x.reshape(2, x.shape[0] // 2, x.shape[1])
    got = swap(take(halves, w[(nt,), 1]), AXES, nt, n)
    own = take(halves, w[(nt,), 0])
    x = (own.astype(f32) + got.astype(f32)).astype(bf16)
    xs = x.reshape(len(found), x.shape[0] // len(found), x.shape[1])
    return [take(xs, w[tuple(near), j]) for j in range(len(found))]


def split_near(pieces, nb, nt):
    found = members([m * nt for m in near_masks(nb)])
    return pieces[:1] + [swap(x, AXES, m, nb * nt) for x, m in zip(pieces[1:], found[1:])]


def join(x, group, w, n):
    found = members(group)
    out = jnp.zeros((len(found),) + x.shape, x.dtype)
    got = [x] + [swap(x, AXES, m, n) for m in found[1:]]
    for j, g in enumerate(got):
        out = put(out, g, w[tuple(group), j])
    return out


def finish_sum(x, nb, nt, w):
    n = nb * nt
    done = []
    for group in far_groups(nb, nt):
        found = members(group)
        size = len(found)
        if x.ndim == 2 or x.shape[0] != size:
            terms = [x.astype(f32)] + [swap(x, AXES, m, n).astype(f32) for m in found[1:]]
            while len(terms) > 1:
                terms = [a + b for a, b in zip(terms[::2], terms[1::2])]
            x = terms[0].astype(bf16)
            continue
        got = [swap(take(x, w[tuple(group), j]), AXES, found[j], n) for j in range(1, size)]
        own = take(x, w[tuple(group), 0]).astype(f32)
        x = sum((g.astype(f32) for g in got), own).astype(bf16)
        done.append(group)
    for group in reversed(done):
        x = join(x, group, w, n)
    found = members([m * nt for m in near_masks(nb)])
    own = [x] + [swap(x, AXES, m, n) for m in found[:0:-1]][::-1]
    return own, [swap(x, AXES, nt, n) for x in own]


def hot(ids, width, dtype):
    return (ids[:, None] == jnp.arange(width, dtype=jnp.int32)[None, :]).astype(dtype)


def nt_dot(a, b):
    return lax.dot_general(a, b, (((1,), (1,)), ((), ())), preferred_element_type=f32)


def tn_dot(a, b, preferred_element_type=f32):
    return lax.dot_general(
        a, b, (((0,), (0,)), ((), ())), preferred_element_type=preferred_element_type
    )


def hot_columns(ids, width):
    found = lax.broadcasted_iota(jnp.int32, (width, ids.shape[1]), 0) == ids
    return jnp.where(found, 1.0, 0.0).astype(bf16)


def gelu_pair(x):
    c = 0.7978845608028654
    square = x * x
    t = jnp.tanh(c * (x + 0.044715 * (square * x)))
    half = 0.5 * (1.0 + t)
    slope = half + (0.5 * x) * ((1.0 - t) * (1.0 + t)) * (c + (3.0 * 0.044715 * c) * square)
    return (x * half).astype(bf16), slope


def forward(rows, one_hot, w_in, bias, w_out, dot=tn_dot):
    embed = w_out.shape[1]
    table = bias[...]
    table = jnp.concatenate([table, jnp.zeros((embed - table.shape[0], table.shape[1]), f32)], 0)
    added = None
    for _ in range(3):
        piece = table.astype(bf16)
        table = table - piece.astype(f32)
        part = dot(one_hot, piece, preferred_element_type=f32)
        added = part if added is None else added + part
    pre = jnp.dot(rows, w_in[...], preferred_element_type=f32) + added
    hidden, slope = gelu_pair(pre)
    latent = jnp.dot(hidden, w_out[...], preferred_element_type=f32)
    radius = jnp.sqrt(jnp.sum(latent * latent, axis=1, keepdims=True) + epsilon)
    return (latent / radius).astype(bf16), latent, hidden, slope, pre


def front_kernel(count, *refs):
    held, (unit_ref, wide_ref), scratch, sems = (
        refs[:count],
        refs[count : count + 2],
        refs[count + 2 : -1],
        refs[-1],
    )
    copies = [
        pltpu.make_async_copy(src, dst, sems.at[i]) for i, (src, dst) in enumerate(zip(held, scratch))
    ]
    for copy in copies:
        copy.start()
    w_in, bias, w_out, ids, rows = scratch
    for copy in copies:
        copy.wait()
    embed, channels = w_out.shape[1], w_in.shape[0]
    one_hot = hot_columns(ids[...], embed)
    unit_ref[...] = forward(rows[...], one_hot, w_in, bias, w_out)[0]
    wide_ref[:, :channels] = rows[...]
    wide_ref[:, channels:] = one_hot.astype(f32).T.astype(bf16)


def refs_kernel(rows, ids, w_in, bias, w_out, unit, latent, hidden, slope):
    values = forward(rows[...], hot_columns(ids[...], w_out.shape[1]), w_in, bias, w_out)
    for out, value in zip((unit, latent, hidden, slope), values):
        out[...] = value


def near_forward_kernel(wide, w_in, bias, w_out, latent, hidden, slope):
    channels = w_in.shape[0]
    values = forward(wide[:, :channels], wide[:, channels:], w_in, bias, w_out, jnp.dot)
    for out, value in zip((latent, hidden, slope), values[1:]):
        out[...] = value


def exponent_kernel(u_ref, pool_ref, exponent_ref):
    scores = nt_dot(u_ref[...], pool_ref[...]) / logit_sharpness_divisor
    exponent_ref[...] = jnp.exp(scores - shift_bound)


def positives_kernel(here_ref, owner, own, ids, w_in, bias, w_out, *refs):
    gots, (rows_ref, unit_ref, latent_ref, pre_ref) = refs[:-4], refs[-4:]
    held = jnp.where(owner[...] == here_ref[0], 1.0, 0.0)
    held = jnp.broadcast_to(held, (w_out.shape[1], held.shape[1])).T[:, :1] > 0.5
    rows = gots[0][...]
    for got in gots[1:]:
        rows = rows + got[...]
    rows = jnp.where(held, own[...].astype(f32), rows.astype(f32)).astype(bf16)
    rows_ref[...] = rows
    values = forward(rows, hot_columns(ids[...], w_out.shape[1]), w_in, bias, w_out)
    unit_ref[...], latent_ref[...], pre_ref[...] = values[0], values[1], values[4]


def score_kernel(scale, order, me_ref, u_ref, v_ref, pool_ref, exponent_ref, *refs):
    kept_ref, sent_ref, loss_ref, grad_ref, grad_pos, share_ref = refs
    v = v_ref[...]
    u, pool = u_ref[...], pool_ref[...]
    uf, vf = u.astype(f32), v.astype(f32)
    pos_score = jnp.sum(uf * vf, axis=1, keepdims=True) / logit_sharpness_divisor
    exponent = exponent_ref[...]
    pos_exp = jnp.exp(pos_score - shift_bound)
    normalizer = pos_exp + jnp.sum(exponent, axis=1, keepdims=True)
    weights = (exponent / normalizer).astype(bf16)
    share_ref[...] = scale * tn_dot(weights, u)
    rows = kept_ref.shape[0] // len(order)
    for i, k in enumerate(order):
        at = pl.multiple_of((me_ref[0] ^ k) * rows, rows)
        kept_ref[i * rows : (i + 1) * rows, :] = share_ref[pl.ds(at, rows), :]
        at = pl.multiple_of((me_ref[0] ^ k ^ 1) * rows, rows)
        sent_ref[i * rows : (i + 1) * rows, :] = share_ref[pl.ds(at, rows), :].astype(bf16)
    loss = jnp.log(normalizer) + shift_bound - pos_score
    loss_ref[...] = jnp.broadcast_to(loss, uf.shape).T[:1]
    pull = pos_exp / normalizer - 1.0
    grad_ref[...] = scale * (jnp.dot(weights, pool, preferred_element_type=f32) + pull * vf)
    grad_pos[...] = scale * pull * uf


def pulled_back(latent, slope, grad_unit, w_out):
    power = jnp.sum(latent * latent, axis=1, keepdims=True) + epsilon
    radius = jnp.sqrt(power)
    inner = jnp.sum(latent * grad_unit, axis=1, keepdims=True)
    grad_latent = ((grad_unit - latent * (inner / (radius * radius))) / radius).astype(bf16)
    return grad_latent, (nt_dot(grad_latent, w_out[...]) * slope).astype(bf16)


def piece_sizes(channels, embed, animals, pieces):
    return channels // (2 * pieces), embed // (2 * pieces), -(-animals // 8) * 8


def two_sets_kernel(
    pieces, animals, ids, a_rows, a_latent, a_hidden, a_slope, a_grad, b_rows, b_latent, b_pre, b_grad, w_out, total
):
    embed, channels = w_out.shape[1], a_rows.shape[1]
    one_hot = hot_columns(ids[...], embed)
    a_latent_grad, a_pre_grad = pulled_back(a_latent[...], a_slope[...], a_grad[...], w_out)
    b_hidden, b_slope = gelu_pair(b_pre[...])
    b_latent_grad, b_pre_grad = pulled_back(b_latent[...], b_slope, b_grad[...], w_out)
    big = tn_dot(a_rows[...], a_pre_grad) + tn_dot(b_rows[...], b_pre_grad)
    low = tn_dot(a_latent_grad, a_hidden[...]) + tn_dot(b_latent_grad, b_hidden)
    animal = jnp.dot(one_hot, a_pre_grad, preferred_element_type=f32)
    animal = animal + jnp.dot(one_hot, b_pre_grad, preferred_element_type=f32)
    top, small, biases = piece_sizes(channels, embed, animals, pieces)
    for i in range(2 * pieces):
        at = i * (top + small + biases)
        total[at : at + top, :] = big[i * top : (i + 1) * top]
        total[at + top : at + top + small, :] = low[i * small : (i + 1) * small]
        total[at + top + small : at + top + small + biases, :] = animal[:biases]


def negatives_kernel(pieces, animals, wide, latent, hidden, slope, grad, w_out, before, total):
    embed = w_out.shape[1]
    channels = wide.shape[1] - embed
    grad_latent, grad_pre = pulled_back(latent[...], slope[...], grad[...], w_out)
    big = tn_dot(wide[:, :channels], grad_pre)
    low = tn_dot(grad_latent, hidden[...])
    animal = tn_dot(wide[:, channels:], grad_pre)
    top, small, biases = piece_sizes(channels, embed, animals, pieces)
    for i in range(2 * pieces):
        at = i * (top + small + biases)
        ends = (at, at + top, at + top + small, at + top + small + biases)
        terms = (big[i * top : (i + 1) * top], low[i * small : (i + 1) * small], animal[:biases])
        for start, end, term in zip(ends, ends[1:], terms):
            total[start:end, :] = (before[start:end, :] + term).astype(bf16)


def piece_kernel(*refs):
    terms, out = refs[:-1], refs[-1]
    got = terms[0][...].astype(f32)
    for term in terms[1:]:
        got = got + term[...].astype(f32)
    blocks, _, width = out.shape
    for i in range(blocks):
        out[i] = got[:, i * width : (i + 1) * width].astype(bf16)


def finish_kernel(pieces, core_ref, *refs):
    places, own, other = (refs[i * pieces : (i + 1) * pieces] for i in range(3))
    grad_w_in, grad_w_out, grad_bias, lows, bias_rows = refs[3 * pieces :]
    animals = grad_bias.shape[0]
    top, small, biases = piece_sizes(grad_w_in.shape[0], grad_w_out.shape[1], animals, pieces)
    blocks, _, width = own[0].shape
    for half, held in ((core_ref[0], own), (1 - core_ref[0], other)):
        for place_ref, piece in zip(places, held):
            at = half * pieces + place_ref[0]
            tops = pl.ds(pl.multiple_of(at * top, top), top)
            rows = pl.ds(pl.multiple_of(at * small, small), small)
            last = pl.ds(pl.multiple_of(at * biases, biases), biases)
            for i in range(blocks):
                columns = slice(i * width, (i + 1) * width)
                grad_w_in[tops, columns] = piece[i, :top, :]
                lows[rows, columns] = piece[i, top : top + small, :].astype(f32)
                bias_rows[last, columns] = piece[i, top + small :, :].astype(f32)
    grad_w_out[...] = lows[...].T
    grad_bias[...] = bias_rows[:animals, :]


def call(kernel, name, out, *args, scalars=0, limit=12, space=pltpu.VMEM, scratch=()):
    whole = pl.BlockSpec(memory_space=pltpu.VMEM)
    given = pl.BlockSpec(memory_space=space)
    shapes = [jax.ShapeDtypeStruct(*o) for o in out]
    return pl.pallas_call(
        kernel,
        name=name,
        out_shape=shapes,
        in_specs=[pl.BlockSpec(memory_space=pltpu.SMEM)] * scalars + [given] * (len(args) - scalars),
        out_specs=[whole] * len(out),
        scratch_shapes=list(scratch),
        compiler_params=pltpu.CompilerParams(vmem_limit_bytes=limit * 2**20),
    )(*args)


def sets(rows, embed, width):
    return [((rows, embed), f32), ((rows, width), bf16), ((rows, width), f32)]


def slots(owner, row, nt, me_t):
    refs = row.shape[0]
    cap = 2 * refs // nt
    owner_hot = hot(owner, nt, jnp.int32)
    slot = jnp.sum((jnp.cumsum(owner_hot, axis=0) - owner_hot) * owner_hot, axis=1)
    found = []
    for k in range(1, nt):
        wanted = owner == (me_t ^ k)
        pick = wanted[None, :] & (slot[None, :] == jnp.arange(cap, dtype=jnp.int32)[:, None])
        found.append((pick, jnp.max(jnp.where(pick, row[None, :], -1), axis=1)[None, :]))
    return found


def pick_kernel(row, recording, rows):
    one_hot = hot_columns(row[...], recording.shape[0])
    rows[...] = tn_dot(one_hot, recording[...]).astype(bf16)


def pick_rows(row, recording):
    out = [((row.shape[1], recording.shape[1]), bf16)]
    return call(pick_kernel, "pick", out, row, recording)[0]


def on_device(
    ref_rows,
    neg_rows,
    recording,
    pos_owner,
    pos_row,
    ref_animal,
    neg_animal,
    w_in,
    bias_animal,
    w_out,
):
    refs = ref_rows.shape[0]
    channels = w_in.shape[0]
    embed = w_out.shape[1]
    animals = bias_animal.shape[0]
    nt = lax.axis_size("tm")
    nb = lax.axis_size("batch")
    n = nt * nb
    me_b = lax.axis_index("batch")
    me_t = lax.axis_index("tm")
    w = positions(nb, nt, me_b, me_t)
    here, *found = lax.optimization_barrier((me_t.reshape(1), *w.values()))
    w = dict(zip(w, found))

    owner, row = pos_owner.reshape(1, refs), pos_row.reshape(1, refs)
    ref_ids, neg_ids = ref_animal[None, :], neg_animal[None, :]
    if nt == 2:
        asks = [(None, row)]
    else:
        asks = slots(pos_owner[:, 0], pos_row, nt, me_t)
    asked = [swap(ask, "tm", k, nt) for k, (_, ask) in enumerate(asks, 1)]
    weights = (w_in, bias_animal, w_out)
    hidden_width = w_in.shape[1]
    inputs = (*weights, neg_ids, neg_rows)
    inputs = [pltpu.with_memory_space_constraint(x, pltpu.HBM) for x in inputs]
    negs = neg_rows.shape[0]
    here, *inputs = lax.optimization_barrier((here, *inputs))
    neg_unit, wide = call(
        functools.partial(front_kernel, len(inputs)),
        "front",
        [((negs, embed), bf16), ((negs, channels + embed), bf16)],
        *inputs,
        space=pltpu.HBM,
        scratch=[pltpu.VMEM(x.shape, x.dtype) for x in inputs]
        + [pltpu.SemaphoreType.DMA((len(inputs),))],
    )
    found = [pick_rows(ask, recording) for ask in asked]
    neg_unit, found, wide = lax.optimization_barrier((neg_unit, found, wide))
    got = [swap(f, "tm", k, nt) for k, f in enumerate(found, 1)]
    near = near_masks(nb)
    shared = wide_masks(nb)
    wide = spread(wide, shared[:1], nb)
    pool, wide, (ref_rows, row) = gather_batch(neg_unit, nb, w, wide, (ref_rows, row))
    wide = spread(wide, shared[1:], nb)
    u, ref_latent, ref_hidden, ref_slope = call(
        refs_kernel,
        "refs",
        [((refs, embed), bf16), *sets(refs, embed, hidden_width)],
        *(ref_rows, ref_ids, *weights),
    )
    own = pick_rows(row, recording)
    got = [
        g if pick is None else jnp.dot(pick.T.astype(bf16), g, preferred_element_type=bf16)
        for (pick, _), g in zip(asks, got)
    ]

    scale = float(refs * n) ** (-0.5) / logit_sharpness_divisor
    exponent = call(
        exponent_kernel,
        "exponents",
        [((refs, pool.shape[0]), f32)],
        *(u, pool),
        limit=max(12, 12 * refs * pool.shape[0] >> 20),
    )[0]
    pos_rows, v, pos_latent, pos_pre = call(
        positives_kernel,
        "positives",
        [(ref_rows.shape, bf16), (u.shape, bf16), (u.shape, f32), ((refs, hidden_width), f32)],
        *(here, owner, own, ref_ids, *weights, *got),
        scalars=1,
    )
    half = pool.shape[0] // 2
    out = [((half, embed), f32), ((half, embed), bf16), ((1, refs), f32)]
    out += [(u.shape, f32), (u.shape, f32)]
    kept, sent, loss, grad_ref, grad_pos = call(
        functools.partial(score_kernel, scale, kept_order(nb)),
        "scores",
        out,
        *(w["b", 0].reshape(1), u, v, pool, exponent),
        scalars=1,
        limit=max(12, 20 * refs * pool.shape[0] >> 20),
        scratch=[pltpu.VMEM((pool.shape[0], embed), f32)],
    )
    pieces = 1 << len(near)
    piece_rows = sum(piece_sizes(channels, embed, animals, pieces))
    total = call(
        functools.partial(two_sets_kernel, pieces, animals),
        "backward",
        [((2 * pieces * piece_rows, hidden_width), f32)],
        ref_ids,
        *(ref_rows, ref_latent, ref_hidden, ref_slope, grad_ref),
        *(pos_rows, pos_latent, pos_pre, grad_pos),
        w_out,
    )[0]
    mine, wide = scatter_batch(kept, sent, nb, wide)
    near_values = call(
        near_forward_kernel,
        "near_forward",
        sets(wide.shape[0], embed, hidden_width),
        *(wide, *weights),
    )
    total = call(
        functools.partial(negatives_kernel, pieces, animals),
        "negatives",
        [(total.shape, bf16)],
        *(wide, *near_values, mine, w_out, total),
    )[0]
    parts = split_pair(total, nb, nt, w)
    total = call(
        piece_kernel,
        "piece",
        [((hidden_width // 128, piece_rows, 128), bf16)],
        *split_near(parts, nb, nt),
    )[0]
    own, other = finish_sum(total, nb, nt, w)
    places = [w[tuple(m * nt for m in near), j].reshape(1) for j in range(pieces)]
    grad_w_in, grad_w_out, grad_bias = call(
        functools.partial(finish_kernel, pieces),
        "finish",
        [(w_in.shape, bf16), (w_out.shape, f32), (bias_animal.shape, f32)],
        w[(nt,), 0].reshape(1),
        *(*places, *own, *other),
        scalars=1 + pieces,
        scratch=[
            pltpu.VMEM((embed, hidden_width), f32),
            pltpu.VMEM((2 * pieces * piece_sizes(channels, embed, animals, pieces)[2], hidden_width), f32),
        ],
    )
    return (loss.reshape(refs), grad_w_in, grad_w_out, grad_bias)


def solution(mesh):
    in_specs = (
        P(("batch", "tm"), None),
        P(("batch", "tm"), None),
        P("tm", None),
        P(("batch", "tm"), None),
        P(("batch", "tm")),
        P(("batch", "tm")),
        P(("batch", "tm")),
        P(),
        P(),
        P(),
    )
    out_specs = (P(("batch", "tm")), P(), P(), P())
    return jax.shard_map(
        on_device, mesh=mesh, in_specs=in_specs, out_specs=out_specs, check_vma=False
    )
```
